32 devices in a mesh: seq: 8 (over z, y), tensor: 4 (over x, core).
Axes of the slice: x: 2, y: 2, z: 4, core: 2. Of those that a mesh axis runs over, the one named last changes fastest.
Arguments:
- block_input: float32 [8192, 1024], P(('seq', 'tensor')), may hold values from -6 to 6
- lengths: int32 [8], replicated, may hold values from 512 to 2048, as said below
- ln_gain: bfloat16 [2, 1024], P(None, ('seq', 'tensor')), may hold values from 0.25 to 1.75
- ln_bias: bfloat16 [2, 1024], P(None, ('seq', 'tensor')), may hold values from -1.5 to 1.5
- qkv_weight: bfloat16 [2, 1024, 3, 1024], P(None, 'seq', None, 'tensor'), may hold values from -0.1875 to 0.1875
- qkv_bias: bfloat16 [2, 3, 16, 64], P(None, None, 'tensor', 'seq'), may hold values from -2.5 to 2.5
- out_weight: bfloat16 [2, 1024, 1024], P(None, 'seq', 'tensor'), may hold values from -0.75 to 0.75
- up_weight: bfloat16 [2, 1024, 4096], P(None, 'seq', 'tensor'), may hold values from -0.1875 to 0.1875
- up_bias: bfloat16 [2, 16, 256], P(None, 'tensor', 'seq'), may hold values from -2.5 to 2.5
- down_weight: bfloat16 [2, 1024, 4096], P(None, 'seq', 'tensor'), may hold values from -0.09375 to 0.09375
- out_bias: bfloat16 [2, 1024], P(None, ('seq', 'tensor')), may hold values from -2.5 to 2.5
- out_grad: float32 [8192, 1024], P(('seq', 'tensor')), may hold values from -6 to 6
Outputs:
- block_output: float32 [8192, 1024], P(('seq', 'tensor'))
- input_grad: float32 [8192, 1024], P(('seq', 'tensor'))
- ln_gain_grad: float32 [2, 1024], P(None, ('seq', 'tensor'))
- ln_bias_grad: float32 [2, 1024], P(None, ('seq', 'tensor'))
- qkv_weight_grad: float32 [2, 1024, 3, 1024], P(None, 'seq', None, 'tensor')
- qkv_bias_grad: float32 [2, 3, 16, 64], P(None, None, 'tensor', 'seq')
- out_weight_grad: float32 [2, 1024, 1024], P(None, 'seq', 'tensor')
- up_weight_grad: float32 [2, 1024, 4096], P(None, 'seq', 'tensor')
- up_bias_grad: float32 [2, 16, 256], P(None, 'tensor', 'seq')
- down_weight_grad: float32 [2, 1024, 4096], P(None, 'seq', 'tensor')
- out_bias_grad: float32 [2, 1024], P(None, ('seq', 'tensor'))
The draws below stay inside these ranges and needn't reach their ends.
Inputs may be any that keep to these rules, and one draw needn't show every extreme that they name: `lengths`: each length is 512, 1024 or 2048; half of them are 512, a quarter 2 * 512 and a quarter 4 * 512, so that they sum to 8192.
All inputs are finite; a program needn't handle non-finite values.
Results may differ from the reference program's by a relative error of at most 0.022.
Values may be sent and summed in bfloat16 or wider, within the bound.
No kernel may reach another device: no remote copies, remote signals or barrier semaphores. Data moves between devices by JAX's collectives and lax.ppermute only.
A program may use at most 256 MiB of HBM per device.

```python
import jax
import jax.numpy as jnp
from jax import lax

D = 1024
HEADS = 16
HEAD_DIM = 64
FF = 4096
ROT = 16
LAYERS = 2
UNIT = 512
TOK_DEV = 1024
TOKENS = 8192
SEQS = 8


def draw_lengths(key, part):
    pattern = jnp.array([1, 1, 2, 4], dtype=jnp.int32)
    units = jnp.tile(pattern, SEQS // 4)
    return (jax.random.permutation(key, units) * UNIT).astype(jnp.int32)


def raised(values, rng, source, target, blocks, factor):
    def block_of(axis_at):
        return (jnp.arange(values.shape[axis_at]) // (values.shape[axis_at] // blocks)).reshape((-1,) + (1,) * (values.ndim - 1 - axis_at))

    one_side = jax.random.permutation(rng, blocks)[block_of(target)]
    far = (block_of(target) + blocks // 2) % blocks
    return jnp.where((block_of(source) == one_side) | (block_of(source) == far), factor * values, values)


def shard_levels(rng, extent, pieces, smallest, largest):
    loudness = 1.0
    for axis_at, shards_of in pieces:
        steps = jax.random.uniform(jax.random.fold_in(jax.random.fold_in(rng, 6), axis_at), (shards_of,), jnp.float32, smallest / len(pieces), largest / len(pieces))
        loudness = loudness * jnp.repeat(jnp.exp(steps), extent[axis_at] // shards_of).reshape((-1,) + (1,) * (len(extent) - 1 - axis_at))
    return loudness


def gaussian(stream_key, dims, width, bound, pieces=(), kind=jnp.bfloat16):
    values = width * jax.random.normal(stream_key, dims, jnp.float32)
    if pieces:
        values = values * shard_levels(stream_key, dims, pieces, -0.22, 0.18)
    return jnp.clip(values, -bound, bound).astype(kind)


def bell_draw_with(own_key, shape, width, bound, shards, heavy, kind=jnp.bfloat16):
    drawn = width * jax.random.normal(own_key, shape, jnp.float32)
    if shards:
        drawn = drawn * shard_levels(own_key, shape, shards, -0.22, 0.18)
    return jnp.clip(raised(drawn, jax.random.fold_in(own_key, 3), *heavy), -bound, bound).astype(kind)


def setup_inputs(seed: int = 0) -> dict:
    streams_of = jax.random.split(jax.random.key(seed), 13)
    block_input = gaussian(streams_of[0], (TOKENS, D), 1.0, 6.0, ((0, 32),), jnp.float32)
    lengths = draw_lengths(jax.random.fold_in(streams_of[12], 71), 0)
    ln_gain = jnp.clip(1.0 + 0.15 * jax.random.normal(streams_of[2], (LAYERS, D), jnp.float32), 0.25, 1.75).astype(jnp.bfloat16)
    ln_bias = gaussian(streams_of[3], (LAYERS, D), 0.3, 1.5, ((1, 32),))
    qkv_weight = gaussian(streams_of[4], (LAYERS, D, 3, D), D ** -0.5, 0.1875, ((1, 8), (3, 4)))
    qkv_bias = gaussian(streams_of[5], (LAYERS, 3, HEADS, HEAD_DIM), 0.5, 2.5, ((2, 4), (3, 8)))
    out_weight = gaussian(streams_of[6], (LAYERS, D, D), (D // 16) ** -0.5, 0.75, ((1, 8), (2, 4)))
    up_weight = gaussian(streams_of[7], (LAYERS, D, FF), D ** -0.5, 0.1875, ((1, 8), (2, 4)))
    up_bias = gaussian(streams_of[8], (LAYERS, HEADS, FF // HEADS), 0.5, 2.5, ((1, 4), (2, 8)))
    down_weight = gaussian(streams_of[9], (LAYERS, D, FF), FF ** -0.5, 0.09375, ((1, 8), (2, 4)))
    out_bias = gaussian(streams_of[10], (LAYERS, D), 0.5, 2.5, ((1, 32),))
    out_grad = bell_draw_with(streams_of[11], (TOKENS, D), 1.0, 6.0, ((0, 32),), (0, 1, 32, 2.75), jnp.float32)
    return {"block_input": block_input, "lengths": lengths, "ln_gain": ln_gain, "ln_bias": ln_bias, "qkv_weight": qkv_weight, "qkv_bias": qkv_bias, "out_weight": out_weight, "up_weight": up_weight, "up_bias": up_bias, "down_weight": down_weight, "out_bias": out_bias, "out_grad": out_grad}


@jax.custom_vjp
def low(v):
    return lax.optimization_barrier(v.astype(jnp.bfloat16)).astype(jnp.float32)

@jax.custom_vjp
def low_back(v):
    return v

def low_keep(v):
    return (low(v), None)

def low_pass(kept, grad):
    return (grad,)

def back_keep(v):
    return (v, None)

def back_low(kept, grad):
    return (low(grad),)
low.defvjp(low_keep, low_pass)
low_back.defvjp(back_keep, back_low)
EPSILON = 1e-05
MASKED = -1e+30
HIGHEST = lax.Precision.HIGHEST

def layer_norm(values, gain, shift):
    center = values - lax.optimization_barrier(jnp.mean(values, axis=1, keepdims=True))
    scale_inv = lax.rsqrt(lax.optimization_barrier(jnp.mean(center * center, axis=1, keepdims=True)) + EPSILON)
    return center * scale_inv * gain + shift

def rotary_tables(offsets):
    exponent = jnp.arange(0, ROT, 2).astype(jnp.float32) / ROT
    angles = offsets.astype(jnp.float32)[:, None] * (10000.0 ** (-exponent))[None, :]
    angles = jnp.concatenate([angles, angles], axis=1)
    return (jnp.cos(angles), jnp.sin(angles))

def rotate(values, cosine, sine):
    half = ROT // 2
    turned = values[..., :ROT]
    swapped = jnp.concatenate([-turned[..., half:], turned[..., :half]], axis=-1)
    rotated = turned * cosine[:, None, :] + swapped * sine[:, None, :]
    return jnp.concatenate([rotated, values[..., ROT:]], axis=-1)

def attention(query, key, value, starts_of):
    group = TOK_DEV
    blocks = TOKENS // group
    padding = jnp.zeros((2 * group, HEADS, HEAD_DIM), query.dtype)
    key_padded = jnp.concatenate([padding, key], axis=0)
    value_padded = jnp.concatenate([padding, value], axis=0)

    def one_block(index):
        begin = index * group
        query_block = lax.dynamic_slice_in_dim(query, begin, group, 0)
        key_block = lax.dynamic_slice_in_dim(key_padded, begin, 3 * group, 0)
        value_block = lax.dynamic_slice_in_dim(value_padded, begin, 3 * group, 0)
        start_block = lax.dynamic_slice_in_dim(starts_of, begin, group, 0)
        query_pos = begin + jnp.arange(group, dtype=jnp.int32)
        key_pos = begin - 2 * group + jnp.arange(3 * group, dtype=jnp.int32)
        visible = (key_pos[None, :] >= start_block[:, None]) & (key_pos[None, :] <= query_pos[:, None])
        scores = jnp.einsum('qhd,khd->hqk', query_block, key_block, precision=HIGHEST) * HEAD_DIM ** (-0.5)
        scores = low_back(scores)
        scores = jnp.where(visible[None], scores, MASKED)
        probs = low(jax.nn.softmax(scores, axis=-1))
        return jnp.einsum('hqk,khd->qhd', probs, value_block, precision=HIGHEST)
    mixed = lax.map(jax.checkpoint(one_block), jnp.arange(blocks, dtype=jnp.int32))
    return mixed.reshape(TOKENS, HEADS, HEAD_DIM)

def reference(block_input, lengths, ln_gain, ln_bias, qkv_weight, qkv_bias, out_weight, up_weight, up_bias, down_weight, out_bias, out_grad):
    positions = jnp.arange(TOKENS, dtype=jnp.int32)
    ends = jnp.cumsum(lengths).astype(jnp.int32)
    starts_of = lax.optimization_barrier(jnp.sum(jnp.where(ends[None, :] <= positions[:, None], lengths[None, :], 0), axis=1)).astype(jnp.int32)
    cosine, sine = rotary_tables(positions - starts_of)
    params = tuple((item.astype(jnp.float32) for item in (ln_gain, ln_bias, qkv_weight, qkv_bias, out_weight, up_weight, up_bias, down_weight, out_bias)))

    def forward(values, weights):
        gains, shifts, joint_weight, joint_bias, mix_weight, rise_weight, rise_bias, fall_weight, final_bias = weights
        for layer in range(LAYERS):
            normed = low(layer_norm(values, gains[layer], shifts[layer]))
            joint = jnp.dot(normed, joint_weight[layer].reshape(D, 3 * D), precision=HIGHEST) + joint_bias[layer].reshape(3 * D)
            joint = low_back(joint).reshape(TOKENS, 3, HEADS, HEAD_DIM)
            query = low(rotate(joint[:, 0], cosine, sine))
            key = low(rotate(joint[:, 1], cosine, sine))
            value = low(joint[:, 2])
            mixed = attention(query, key, value, starts_of)
            mixed = low(low_back(mixed)).reshape(TOKENS, D)
            attended = jnp.dot(mixed, mix_weight[layer].T, precision=HIGHEST)
            rise = jnp.dot(normed, rise_weight[layer], precision=HIGHEST) + rise_bias[layer].reshape(FF)
            rise = low_back(rise)
            hidden = low(jax.nn.gelu(rise, approximate=False))
            fallen = jnp.dot(hidden, fall_weight[layer].T, precision=HIGHEST)
            values = values + low_back(attended + fallen) + final_bias[layer]
        return values
    output, pullback = jax.vjp(forward, block_input.astype(jnp.float32), params)
    input_grad, grads = pullback(out_grad.astype(jnp.float32))
    return (output, input_grad, grads[0], grads[1], grads[2], grads[3], grads[4], grads[5], grads[6], grads[7], grads[8])
```

```python
import functools
import jax
import jax.numpy as jnp
from jax import lax
from jax.experimental import pallas as pl
from jax.experimental.pallas import tpu as pltpu
from jax.sharding import PartitionSpec as P

HEAD_DIM = 64
ROT = 16
UNIT = 512
LANES = 128
PAIR = 2 * LANES
EPSILON = 1e-05
MASKED = -1e30
BF = jnp.bfloat16
F32 = jnp.float32


def dot_nn(left, right):
    return lax.dot_general(left, right, (((1,), (0,)), ((), ())), preferred_element_type=F32)


def dot_nt(left, right):
    return lax.dot_general(left, right, (((1,), (1,)), ((), ())), preferred_element_type=F32)


def dot_tn(left, right):
    return lax.dot_general(left, right, (((0,), (0,)), ((), ())), preferred_element_type=F32)


def turned(values, cosine, sine_low, sine_high):
    ahead = pltpu.roll(values, LANES - ROT // 2, 1)
    behind = pltpu.roll(values, ROT // 2, 1)
    return values * cosine + ahead * sine_low + behind * sine_high


def turned_back(grad, cosine, sine_low, sine_high):
    ahead = pltpu.roll(grad, LANES - ROT // 2, 1)
    behind = pltpu.roll(grad, ROT // 2, 1)
    return grad * cosine - ahead * sine_low - behind * sine_high


def qkv_kernel(x_ref, w_ref, b_ref, c_ref, s1_ref, s2_ref, q_ref, kv_ref, tail_ref):
    joint = dot_nn(x_ref[...], w_ref[...]) + b_ref[...]
    cosine, low, high = c_ref[...], s1_ref[...], s2_ref[...]
    pairs = q_ref.shape[1] // LANES
    for pair in range(pairs):
        lanes = slice(pair * LANES, (pair + 1) * LANES)
        query = turned(joint[:, lanes], cosine, low, high) * HEAD_DIM**-0.5
        q_ref[:, lanes] = query.astype(BF)
        at = (pairs + pair) * LANES
        key = turned(joint[:, at : at + LANES], cosine, low, high).astype(BF)
        at = (2 * pairs + pair) * LANES
        value = joint[:, at : at + LANES].astype(BF)
        kv_ref[0, pair, :, :LANES] = key
        kv_ref[0, pair, :, LANES:] = value
        tail_ref[pair, :, :LANES] = key
        tail_ref[pair, :, LANES:] = value


def qkv_call(normed, weight, bias, tables):
    rows, width = normed.shape
    cols = weight.shape[1]
    head_width = cols // 3
    pairs = head_width // LANES
    blocks = rows // UNIT
    tile = 256
    per = UNIT // tile
    row_spec = pl.BlockSpec((tile, LANES), lambda m: (m, 0))
    first_tail = (blocks - 1) * per
    return pl.pallas_call(
        qkv_kernel,
        grid=(rows // tile,),
        in_specs=[
            pl.BlockSpec((tile, width), lambda m: (m, 0)),
            pl.BlockSpec((width, cols), lambda m: (0, 0)),
            pl.BlockSpec((1, cols), lambda m: (0, 0)),
            row_spec,
            row_spec,
            row_spec,
        ],
        out_specs=[
            pl.BlockSpec((tile, head_width), lambda m: (m, 0)),
            pl.BlockSpec((1, pairs, tile, PAIR), lambda m: (m // per, 0, m % per, 0)),
            pl.BlockSpec((pairs, tile, PAIR), lambda m: (0, jnp.maximum(m - first_tail, 0), 0)),
        ],
        out_shape=[
            jax.ShapeDtypeStruct((rows, head_width), BF),
            jax.ShapeDtypeStruct((blocks, pairs, UNIT, PAIR), BF),
            jax.ShapeDtypeStruct((pairs, UNIT, PAIR), BF),
        ],
        name="qkv",
    )(normed, weight, bias, *tables)


def fill_window(far, near, own, window, at):
    lanes = slice(at, at + LANES)
    window[0:UNIT] = far[0, :, lanes]
    for block in range(2):
        window[(1 + block) * UNIT : (2 + block) * UNIT] = near[block, 0, :, lanes]
        window[(3 + block) * UNIT : (4 + block) * UNIT] = own[block, 0, :, lanes]


def half_of(values, head):
    lane = lax.broadcasted_iota(jnp.int32, values.shape, 1)
    return jnp.where((lane >= HEAD_DIM) == bool(head), values, jnp.zeros_like(values))


def fwd_kernel(n_ref, q_ref, own_ref, near_ref, far_ref, o_ref, lse_ref, kw, vw, vt):
    fill_window(far_ref, near_ref, own_ref, kw, 0)
    fill_window(far_ref, near_ref, own_ref, vw, LANES)
    for block in range(5):
        rows = slice(block * UNIT, (block + 1) * UNIT)
        vt[:, rows] = vw[rows].T
    key_at = lax.broadcasted_iota(jnp.int32, (UNIT, UNIT), 0)
    query_at = lax.broadcasted_iota(jnp.int32, (UNIT, UNIT), 1)
    for block in range(2):
        rows = slice(block * UNIT, (block + 1) * UNIT)
        outs = []
        for head in range(2):
            query = half_of(q_ref[rows, :], head)
            part = slice(head * HEAD_DIM, (head + 1) * HEAD_DIM)
            at = (3 + block) * UNIT
            score = dot_nt(kw[at : at + UNIT], query)
            score = jnp.where(key_at <= query_at, score, MASKED)
            top = jnp.max(score, axis=0, keepdims=True)
            probs = jnp.exp(score - top)
            total = jnp.sum(probs, axis=0, keepdims=True)
            acc = dot_nn(vt[part, at : at + UNIT], probs.astype(BF))

            def step(back, carry, query=query, at=at, part=part):
                top, total, acc = carry
                where = pl.ds(pl.multiple_of(at - back * UNIT, UNIT), UNIT)
                score = dot_nt(kw[where], query)
                higher = jnp.maximum(top, jnp.max(score, axis=0, keepdims=True))
                shrink = jnp.exp(top - higher)
                probs = jnp.exp(score - higher)
                total = total * shrink + jnp.sum(probs, axis=0, keepdims=True)
                acc = acc * shrink + dot_nn(vt[part, where], probs.astype(BF))
                return higher, total, acc

            top, total, acc = lax.fori_loop(1, n_ref[block], step, (top, total, acc))
            outs.append(acc * (1.0 / total))
            lse_ref[0, head : head + 1, rows] = top + jnp.log(total)
        o_ref[rows, :] = jnp.concatenate(outs, axis=0).T.astype(BF)


def window_specs(rows, pairs):
    blocks = rows // UNIT
    kv_spec = pl.BlockSpec((blocks, 1, UNIT, PAIR), lambda p, n: (0, p, 0, 0))
    far_spec = pl.BlockSpec((1, UNIT, PAIR), lambda p, n: (p, 0, 0))
    row_spec = pl.BlockSpec((rows, LANES), lambda p, n: (0, p))
    return row_spec, kv_spec, far_spec


def fwd_call(counts, query, own, near, far):
    rows, head_width = query.shape
    pairs = head_width // LANES
    row_spec, kv_spec, far_spec = window_specs(rows, pairs)
    return pl.pallas_call(
        fwd_kernel,
        grid_spec=pltpu.PrefetchScalarGridSpec(
            num_scalar_prefetch=1,
            grid=(pairs,),
            in_specs=[row_spec, kv_spec, kv_spec, far_spec],
            out_specs=[row_spec, pl.BlockSpec((1, 2, rows), lambda p, n: (p, 0, 0))],
            scratch_shapes=[pltpu.VMEM((5 * UNIT, LANES), BF)] * 2
            + [pltpu.VMEM((LANES, 5 * UNIT), BF)],
        ),
        out_shape=[
            jax.ShapeDtypeStruct((rows, head_width), BF),
            jax.ShapeDtypeStruct((pairs, 2, rows), F32),
        ],
        name="attend",
    )(counts, query, own, near, far)


def bwd_kernel(
    n_ref, q_ref, own_ref, near_ref, far_ref, o_ref, do_ref, lse_ref, c_ref, s1_ref, s2_ref,
    dq_ref, down_ref, dnear_ref, dfar_ref, kw, vw, kt, dk, dv, dqt,
):
    fill_window(far_ref, near_ref, own_ref, kw, 0)
    fill_window(far_ref, near_ref, own_ref, vw, LANES)
    for block in range(5):
        rows = slice(block * UNIT, (block + 1) * UNIT)
        kt[:, rows] = kw[rows].T
    dk[...] = jnp.zeros_like(dk)
    dv[...] = jnp.zeros_like(dv)
    lane = lax.broadcasted_iota(jnp.int32, (UNIT, LANES), 1)
    key_at = lax.broadcasted_iota(jnp.int32, (UNIT, UNIT), 0)
    query_at = lax.broadcasted_iota(jnp.int32, (UNIT, UNIT), 1)
    for block in range(2):
        rows = slice(block * UNIT, (block + 1) * UNIT)
        grad = do_ref[rows, :]
        both = grad.astype(F32) * o_ref[rows, :].astype(F32)
        delta0 = jnp.sum(jnp.where(lane < HEAD_DIM, both, 0.0), axis=1, keepdims=True)
        delta1 = jnp.sum(jnp.where(lane < HEAD_DIM, 0.0, both), axis=1, keepdims=True)
        deltas = jnp.where(lane == 0, delta0, delta1).T
        dqt[...] = jnp.zeros_like(dqt)
        for head in range(2):
            query = half_of(q_ref[rows, :], head)
            grad_half = half_of(grad, head)
            lse = lse_ref[0, head : head + 1, rows]
            delta = deltas[head : head + 1, :]
            part = slice(head * HEAD_DIM, (head + 1) * HEAD_DIM)

            def visit(start, masked, query=query, grad_half=grad_half, lse=lse, delta=delta, part=part):
                where = pl.ds(start, UNIT)
                score = dot_nt(kw[where], query)
                if masked:
                    score = jnp.where(key_at <= query_at, score, MASKED)
                probs = jnp.exp(score - lse)
                probs_grad = dot_nt(vw[where], grad_half)
                score_grad = (probs * (probs_grad - delta)).astype(BF)
                dv[where] += dot_nn(probs.astype(BF), grad_half)
                dk[where] += dot_nn(score_grad, query)
                dqt[part, :] += dot_nn(kt[part, where], score_grad)

            at = (3 + block) * UNIT
            visit(at, True)

            def step(back, carry, at=at, visit=visit):
                visit(pl.multiple_of(at - back * UNIT, UNIT), False)
                return carry

            lax.fori_loop(1, n_ref[block], step, 0)
        dq = dqt[...].T * HEAD_DIM**-0.5
        dq_ref[rows, :] = turned_back(dq, c_ref[rows, :], s1_ref[rows, :], s2_ref[rows, :]).astype(BF)
    for source, at in ((dk, 0), (dv, LANES)):
        lanes = slice(at, at + LANES)
        dfar_ref[0, :, lanes] = source[0:UNIT].astype(BF)
        for block in range(2):
            dnear_ref[block, 0, :, lanes] = source[(1 + block) * UNIT : (2 + block) * UNIT].astype(BF)
            down_ref[block, 0, :, lanes] = source[(3 + block) * UNIT : (4 + block) * UNIT]


def bwd_call(counts, query, own, near, far, out, out_grad, lse, tables):
    rows, head_width = query.shape
    pairs = head_width // LANES
    blocks = rows // UNIT
    row_spec, kv_spec, far_spec = window_specs(rows, pairs)
    table_spec = pl.BlockSpec((rows, LANES), lambda p, n: (0, 0))
    return pl.pallas_call(
        bwd_kernel,
        grid_spec=pltpu.PrefetchScalarGridSpec(
            num_scalar_prefetch=1,
            grid=(pairs,),
            in_specs=[row_spec, kv_spec, kv_spec, far_spec, row_spec, row_spec]
            + [pl.BlockSpec((1, 2, rows), lambda p, n: (p, 0, 0))]
            + [table_spec] * 3,
            out_specs=[row_spec, kv_spec, kv_spec, far_spec],
            scratch_shapes=[pltpu.VMEM((5 * UNIT, LANES), BF)] * 2
            + [pltpu.VMEM((LANES, 5 * UNIT), BF)]
            + [pltpu.VMEM((5 * UNIT, LANES), F32)] * 2
            + [pltpu.VMEM((LANES, UNIT), F32)],
        ),
        out_shape=[
            jax.ShapeDtypeStruct((rows, head_width), BF),
            jax.ShapeDtypeStruct((blocks, pairs, UNIT, PAIR), F32),
            jax.ShapeDtypeStruct((blocks, pairs, UNIT, PAIR), BF),
            jax.ShapeDtypeStruct((pairs, UNIT, PAIR), BF),
        ],
        name="attend_back",
    )(counts, query, own, near, far, out, out_grad, lse, *tables)


def join_kernel(dq_ref, own_ref, near_ref, far_ref, c_ref, s1_ref, s2_ref, jg_ref, sum_ref):
    block = pl.program_id(0)
    cosine, low, high = c_ref[...], s1_ref[...], s2_ref[...]
    pairs = dq_ref.shape[1] // LANES
    last = (block == pl.num_programs(0) - 1).astype(F32)
    parts = [dq_ref[:, p * LANES : (p + 1) * LANES] for p in range(pairs)]
    for at in (0, LANES):
        for pair in range(pairs):
            lanes = slice(at, at + LANES)
            grad = own_ref[0, pair, :, lanes] + near_ref[0, pair, :, lanes].astype(F32)
            grad = grad + last * far_ref[pair, :, lanes].astype(F32)
            if at == 0:
                grad = turned_back(grad, cosine, low, high)
            parts.append(grad.astype(BF))
    for index, part in enumerate(parts):
        lanes = slice(index * LANES, (index + 1) * LANES)
        jg_ref[:, lanes] = part
        column = jnp.sum(part.astype(F32), axis=0, keepdims=True)

        @pl.when(block == 0)
        def _():
            sum_ref[:, lanes] = column

        @pl.when(block > 0)
        def _():
            sum_ref[:, lanes] += column


def join_call(dq, own, near, far, tables):
    rows, head_width = dq.shape
    pairs = head_width // LANES
    blocks = rows // UNIT
    table_spec = pl.BlockSpec((UNIT, LANES), lambda b: (b, 0))
    kv_spec = pl.BlockSpec((1, pairs, UNIT, PAIR), lambda b: (b, 0, 0, 0))
    return pl.pallas_call(
        join_kernel,
        grid=(blocks,),
        in_specs=[
            pl.BlockSpec((UNIT, head_width), lambda b: (b, 0)),
            kv_spec,
            kv_spec,
            pl.BlockSpec((pairs, UNIT, PAIR), lambda b: (0, 0, 0)),
        ]
        + [table_spec] * 3,
        out_specs=[
            pl.BlockSpec((UNIT, 3 * head_width), lambda b: (b, 0)),
            pl.BlockSpec((1, 3 * head_width), lambda b: (0, 0)),
        ],
        out_shape=[
            jax.ShapeDtypeStruct((rows, 3 * head_width), BF),
            jax.ShapeDtypeStruct((1, 3 * head_width), F32),
        ],
        name="join",
    )(dq, own, near, far, *tables)


def up_kernel(x_ref, w_ref, b_ref, hidden_ref, slope_ref):
    rise = dot_nn(x_ref[...], w_ref[...]) + b_ref[...]
    phi = 0.5 + 0.5 * lax.erf(rise * 0.7071067811865476)
    bell = jnp.exp(rise * rise * -0.5) * 0.3989422804014327
    hidden_ref[...] = (rise * phi).astype(BF)
    slope_ref[...] = phi + rise * bell


def up_call(normed, weight, bias):
    rows, width = normed.shape
    cols = weight.shape[1]
    tile = 256
    return pl.pallas_call(
        up_kernel,
        grid=(rows // tile,),
        in_specs=[
            pl.BlockSpec((tile, width), lambda m: (m, 0)),
            pl.BlockSpec((width, cols), lambda m: (0, 0)),
            pl.BlockSpec((1, cols), lambda m: (0, 0)),
        ],
        out_specs=[pl.BlockSpec((tile, cols), lambda m: (m, 0))] * 2,
        out_shape=[
            jax.ShapeDtypeStruct((rows, cols), BF),
            jax.ShapeDtypeStruct((rows, cols), F32),
        ],
        name="up",
    )(normed, weight, bias)


def flipped(count, bit):
    return [(i, i ^ bit) for i in range(count)]


def shifted(count, distance):
    devices = range(count)
    return [(i - distance, i) for i in devices if i - distance in devices]


def rolled_outer(outer, distance):
    return [
        (o * 2 + y, (o + distance) % outer * 2 + y) for o in range(outer) for y in range(2)
    ]


def gather_rows(piece):
    count = lax.axis_size("seq")
    outer = count // 2
    place = lax.axis_index("seq")
    at, side = place // 2, place % 2
    chunk, cols = piece.shape
    line = jnp.zeros((outer, chunk, cols), piece.dtype)
    line = lax.dynamic_update_index_in_dim(line, piece, at, 0)
    for distance in range(1, outer):
        came = lax.ppermute(piece, "seq", rolled_outer(outer, distance))
        line = lax.dynamic_update_index_in_dim(line, came, (at - distance) % outer, 0)
    other = lax.ppermute(line, "seq", flipped(count, 1))
    full = jnp.zeros((outer, 2, chunk, cols), piece.dtype)
    full = lax.dynamic_update_index_in_dim(full, line, side, 1)
    full = lax.dynamic_update_index_in_dim(full, other, 1 - side, 1)
    return full.reshape(count * chunk, cols)


def gather_rows_whole(piece):
    return lax.all_gather(piece, "seq", axis=0, tiled=True)


def halves(values):
    count = lax.axis_size("seq")
    side = lax.axis_index("seq") % 2
    rows, width = values.shape
    split = values.reshape(rows, count // 2, 2, width // count)
    mine = lax.dynamic_index_in_dim(split, side, 2, keepdims=False)
    other = lax.dynamic_index_in_dim(split, 1 - side, 2, keepdims=False)
    return mine.reshape(rows, width // 2), other.reshape(rows, width // 2)


def scatter_grad(left, right):
    count = lax.axis_size("seq")
    outer = count // 2
    at = lax.axis_index("seq") // 2
    mine, other = left
    sent = dot_tn(other, right).astype(BF)
    came = lax.ppermute(sent, "seq", flipped(count, 1))
    paired = (dot_tn(mine, right) + came.astype(F32)).astype(BF)
    line = paired.reshape(outer, -1, right.shape[1])
    total = lax.dynamic_index_in_dim(line, at, 0, keepdims=False).astype(F32)
    for distance in range(1, outer):
        part = lax.dynamic_index_in_dim(line, (at + distance) % outer, 0, keepdims=False)
        part = lax.ppermute(part, "seq", rolled_outer(outer, distance))
        total = total + part.astype(F32)
    return total


def gather_tokens(rows):
    count = lax.axis_size("tensor")
    me = lax.axis_index("tensor")
    across = lax.ppermute(rows, "tensor", flipped(count, 2))
    beside = lax.ppermute(rows, "tensor", flipped(count, 1))
    diagonal = lax.ppermute(across, "tensor", flipped(count, 1))
    out = jnp.zeros((count,) + rows.shape, rows.dtype)
    out = lax.dynamic_update_index_in_dim(out, rows, me, 0)
    out = lax.dynamic_update_index_in_dim(out, beside, me ^ 1, 0)
    out = lax.dynamic_update_index_in_dim(out, across, me ^ 2, 0)
    out = lax.dynamic_update_index_in_dim(out, diagonal, me ^ 3, 0)
    return out.reshape(count * rows.shape[0], rows.shape[1])


def scatter_tokens(partial):
    count = lax.axis_size("tensor")
    me = lax.axis_index("tensor")
    core, chip = me % 2, me // 2
    split = partial.reshape(2, 2, partial.shape[0] // count, partial.shape[1])
    sent = lax.dynamic_index_in_dim(split, 1 - core, 1, keepdims=False)
    kept = lax.dynamic_index_in_dim(split, core, 1, keepdims=False)
    came = lax.ppermute(sent, "tensor", flipped(count, 1))
    far = lax.dynamic_index_in_dim(kept, 1 - chip, 0, keepdims=False).astype(F32)
    far = far + lax.dynamic_index_in_dim(came, 1 - chip, 0, keepdims=False).astype(F32)
    across = lax.ppermute(far.astype(BF), "tensor", flipped(count, 2))
    near = lax.dynamic_index_in_dim(kept, chip, 0, keepdims=False).astype(F32)
    near = near + lax.dynamic_index_in_dim(came, chip, 0, keepdims=False).astype(F32)
    return near + across.astype(F32)


def exchanged(rows):
    return lax.all_to_all(rows, ("seq", "tensor"), 0, 0, tiled=True)


def layer_norm(values, gain, shift):
    center = values - jnp.mean(values, axis=1, keepdims=True)
    scale_inv = lax.rsqrt(jnp.mean(center * center, axis=1, keepdims=True) + EPSILON)
    unit = center * scale_inv
    return (unit * gain + shift, unit, scale_inv)


def norm_back(grad, unit, scale_inv, gain):
    scaled = grad * gain
    return scale_inv * (
        scaled
        - jnp.mean(scaled, axis=1, keepdims=True)
        - unit * jnp.mean(scaled * unit, axis=1, keepdims=True)
    )


def rotary_tables(offsets):
    exponent = jnp.arange(0, ROT, 2).astype(F32) / ROT
    rates = 10000.0 ** (-exponent)
    head = jnp.concatenate([rates, rates, jnp.zeros(HEAD_DIM - ROT, F32)])
    lane = jnp.arange(LANES) % HEAD_DIM
    angles = offsets.astype(F32)[:, None] * jnp.concatenate([head, head])[None, :]
    sine = jnp.sin(angles)
    low = jnp.where(lane < ROT // 2, -sine, 0.0)
    high = jnp.where((lane >= ROT // 2) & (lane < ROT), sine, 0.0)
    return (jnp.cos(angles), low, high)


def local(
    block_input,
    lengths,
    ln_gain,
    ln_bias,
    qkv_weight,
    qkv_bias,
    out_weight,
    up_weight,
    up_bias,
    down_weight,
    out_bias,
    out_grad,
):
    tensor_count = lax.axis_size("tensor")
    seq_count = lax.axis_size("seq")
    everyone = seq_count * tensor_count
    me_tensor = lax.axis_index("tensor")
    own_rows, width = block_input.shape
    group = own_rows * tensor_count
    layers = qkv_weight.shape[0]
    chunk = qkv_weight.shape[1]
    head_width = qkv_weight.shape[3]
    heads = head_width // HEAD_DIM
    hidden_width = up_weight.shape[2]
    first = lax.axis_index("seq") * group
    positions = first + jnp.arange(group, dtype=jnp.int32)
    ends = jnp.cumsum(lengths)
    starts_of = jnp.sum(jnp.where(ends[None, :] <= positions[:, None], lengths[None, :], 0), axis=1)
    offsets = positions - starts_of
    tables = rotary_tables(offsets)
    counts = offsets[::UNIT] // UNIT + 1

    small_sizes = []
    pieces = []
    for array in (ln_gain, ln_bias, out_bias, qkv_bias, up_bias):
        pieces.append(array.reshape(-1))
        small_sizes.append(array.size)
    packed = jnp.concatenate(pieces)
    small = exchanged(jnp.broadcast_to(packed[None, :], (everyone, packed.size)))
    parts = []
    at = 0
    for size in small_sizes:
        parts.append(small[:, at : at + size])
        at += size

    def over_all(part):
        return jnp.transpose(part.reshape(everyone, layers, -1), (1, 0, 2)).reshape(layers, width)

    def over_seq(part):
        part = part.reshape(seq_count, tensor_count, -1)
        return lax.dynamic_index_in_dim(part, me_tensor, 1, keepdims=False)

    gains = over_all(parts[0]).astype(F32)
    shifts = over_all(parts[1]).astype(F32)
    out_biases = over_all(parts[2]).astype(F32)
    per = HEAD_DIM // seq_count
    joint_bias = over_seq(parts[3]).reshape(seq_count, layers, 3, heads, per)
    joint_bias = jnp.transpose(joint_bias, (1, 2, 3, 0, 4)).reshape(layers, 1, 3 * head_width)
    joint_bias = joint_bias.astype(F32)
    groups = up_bias.shape[1]
    rise_bias = over_seq(parts[4]).reshape(seq_count, layers, groups, -1)
    rise_bias = jnp.transpose(rise_bias, (1, 2, 0, 3)).reshape(layers, 1, hidden_width).astype(F32)

    weights = []
    for layer in range(layers):
        gather = GATHER[layer]
        weights.append(
            (
                gather(qkv_weight[layer].reshape(chunk, 3 * head_width)),
                gather(up_weight[layer]),
                gather(jnp.concatenate([out_weight[layer], down_weight[layer]], axis=1)),
            )
        )

    kept = []
    current = block_input
    for layer in range(layers):
        qkv_full, up_full, fall_full = weights[layer]
        normed, unit, scale_inv = layer_norm(current, gains[layer][None], shifts[layer][None])
        normed_rows = gather_tokens(normed.astype(BF))
        query, own, tail = qkv_call(normed_rows, qkv_full, joint_bias[layer], tables)
        near = lax.ppermute(own, "seq", shifted(seq_count, 1))
        far = lax.ppermute(tail, "seq", shifted(seq_count, 2))
        hidden, slope = up_call(normed_rows, up_full, rise_bias[layer])
        mixed, lse = fwd_call(counts, query, own, near, far)
        partial = dot_nt(mixed, fall_full[:, :head_width]) + dot_nt(hidden, fall_full[:, head_width:])
        branch = scatter_tokens(partial.astype(BF))
        kept.append((normed_rows, unit, scale_inv, query, own, near, far, hidden, slope, mixed, lse))
        current = current + branch + out_biases[layer][None, :]

    gradient = out_grad
    collected = []
    for layer in reversed(range(layers)):
        qkv_full, up_full, fall_full = weights[layer]
        normed_rows, unit, scale_inv, query, own, near, far, hidden, slope, mixed, lse = kept[layer]
        bias_grad = jnp.sum(gradient, axis=0)
        grad_rows = gather_tokens(gradient.astype(BF))
        grad_halves = halves(grad_rows)
        normed_halves = halves(normed_rows)
        mixed_grad = dot_nn(grad_rows, fall_full[:, :head_width]).astype(BF)
        fall_grad = scatter_grad(grad_halves, jnp.concatenate([mixed, hidden], axis=1))
        dq, down, dnear, dfar = bwd_call(counts, query, own, near, far, mixed, mixed_grad, lse, tables)
        came_near = lax.ppermute(dnear, "seq", shifted(seq_count, -1))
        came_far = lax.ppermute(dfar, "seq", shifted(seq_count, -2))
        hidden_grad = dot_nn(grad_rows, fall_full[:, head_width:])
        rise_grad = (hidden_grad * slope).astype(BF)
        rise_bias_grad = jnp.sum(rise_grad, axis=0, dtype=F32)
        up_grad = scatter_grad(normed_halves, rise_grad)
        normed_part = dot_nt(rise_grad, up_full)
        joint_grad, joint_bias_grad = join_call(dq, down, came_near, came_far, tables)
        joint_weight_grad = scatter_grad(normed_halves, joint_grad)
        normed_part = normed_part + dot_nt(joint_grad, qkv_full)
        normed_grad = scatter_tokens(normed_part.astype(BF))
        gain_grad = jnp.sum(normed_grad * unit, axis=0)
        shift_grad = jnp.sum(normed_grad, axis=0)
        gradient = gradient + norm_back(normed_grad, unit, scale_inv, gains[layer][None, :])
        collected.append(
            (gain_grad, shift_grad, bias_grad, joint_bias_grad.reshape(-1), rise_bias_grad,
             joint_weight_grad, fall_grad, up_grad)
        )
    collected = collected[::-1]

    def stacked(member):
        return jnp.stack([entry[member] for entry in collected])

    def to_all(member):
        value = stacked(member).reshape(layers, everyone, -1)
        return jnp.transpose(value, (1, 0, 2)).reshape(everyone, -1)

    def to_seq(value):
        mine = jnp.arange(tensor_count)[None, :, None] == me_tensor
        return jnp.where(mine, value[:, None, :], 0.0).reshape(everyone, -1)

    joint_out = stacked(3).reshape(layers, 3, heads, seq_count, per)
    joint_out = jnp.transpose(joint_out, (3, 0, 1, 2, 4)).reshape(seq_count, -1)
    rise_out = stacked(4).reshape(layers, groups, seq_count, -1)
    rise_out = jnp.transpose(rise_out, (2, 0, 1, 3)).reshape(seq_count, -1)
    outgoing = jnp.concatenate(
        [to_all(0), to_all(1), to_all(2), to_seq(joint_out), to_seq(rise_out)], axis=1
    )
    summed = jnp.sum(exchanged(outgoing), axis=0)
    results = []
    at = 0
    for array in (ln_gain, ln_bias, out_bias, qkv_bias, up_bias):
        results.append(summed[at : at + array.size].reshape(array.shape))
        at += array.size
    joint_weight_grad = stacked(5).reshape(layers, chunk, 3, head_width)
    fall_grad = stacked(6)
    return (
        current,
        gradient,
        results[0],
        results[1],
        joint_weight_grad,
        results[3],
        fall_grad[:, :, :head_width],
        stacked(7),
        results[4],
        fall_grad[:, :, head_width:],
        results[2],
    )


GATHER = (gather_rows, gather_rows)


def solution(mesh):
    tokens = P(("seq", "tensor"), None)
    vector = P(None, ("seq", "tensor"))
    matrix = P(None, "seq", "tensor")
    joint = P(None, "seq", None, "tensor")
    joint_vector = P(None, None, "tensor", "seq")
    rise_vector = P(None, "tensor", "seq")
    in_specs = (
        tokens, P(), vector, vector, joint, joint_vector, matrix, matrix, rise_vector, matrix,
        vector, tokens,
    )
    out_specs = (
        tokens, tokens, vector, vector, joint, joint_vector, matrix, matrix, rise_vector, matrix,
        vector,
    )
    return jax.shard_map(local, mesh=mesh, in_specs=in_specs, out_specs=out_specs, check_vma=False)
```

```python
import functools
import jax
import jax.numpy as jnp
from jax import lax
from jax.experimental import pallas as pl
from jax.experimental.pallas import tpu as pltpu
from jax.sharding import PartitionSpec as P

HEAD_DIM = 64
ROT = 16
UNIT = 512
LANES = 128
PAIR = 2 * LANES
EPSILON = 1e-05
MASKED = -1e30
BF = jnp.bfloat16
F32 = jnp.float32


def dot_nn(left, right):
    return lax.dot_general(left, right, (((1,), (0,)), ((), ())), preferred_element_type=F32)


def dot_nt(left, right):
    return lax.dot_general(left, right, (((1,), (1,)), ((), ())), preferred_element_type=F32)


def dot_tn(left, right):
    return lax.dot_general(left, right, (((0,), (0,)), ((), ())), preferred_element_type=F32)


def turned(values, cosine, sine_low, sine_high):
    ahead = pltpu.roll(values, LANES - ROT // 2, 1)
    behind = pltpu.roll(values, ROT // 2, 1)
    return values * cosine + ahead * sine_low + behind * sine_high


def turned_back(grad, cosine, sine_low, sine_high):
    ahead = pltpu.roll(grad, LANES - ROT // 2, 1)
    behind = pltpu.roll(grad, ROT // 2, 1)
    return grad * cosine - ahead * sine_low - behind * sine_high


def qkv_kernel(x_ref, w_ref, b_ref, c_ref, s1_ref, s2_ref, q_ref, kv_ref, tail_ref):
    joint = dot_nn(x_ref[...], w_ref[...]) + b_ref[...]
    cosine, low, high = c_ref[...], s1_ref[...], s2_ref[...]
    pairs = q_ref.shape[1] // LANES
    for pair in range(pairs):
        lanes = slice(pair * LANES, (pair + 1) * LANES)
        query = turned(joint[:, lanes], cosine, low, high) * HEAD_DIM**-0.5
        q_ref[:, lanes] = query.astype(BF)
        at = (pairs + pair) * LANES
        key = turned(joint[:, at : at + LANES], cosine, low, high).astype(BF)
        at = (2 * pairs + pair) * LANES
        value = joint[:, at : at + LANES].astype(BF)
        kv_ref[0, pair, :, :LANES] = key
        kv_ref[0, pair, :, LANES:] = value
        tail_ref[pair, :, :LANES] = key
        tail_ref[pair, :, LANES:] = value


def qkv_call(normed, weight, bias, tables):
    rows, width = normed.shape
    cols = weight.shape[1]
    head_width = cols // 3
    pairs = head_width // LANES
    blocks = rows // UNIT
    tile = 256
    per = UNIT // tile
    row_spec = pl.BlockSpec((tile, LANES), lambda m: (m, 0))
    first_tail = (blocks - 1) * per
    return pl.pallas_call(
        qkv_kernel,
        grid=(rows // tile,),
        in_specs=[
            pl.BlockSpec((tile, width), lambda m: (m, 0)),
            pl.BlockSpec((width, cols), lambda m: (0, 0)),
            pl.BlockSpec((1, cols), lambda m: (0, 0)),
            row_spec,
            row_spec,
            row_spec,
        ],
        out_specs=[
            pl.BlockSpec((tile, head_width), lambda m: (m, 0)),
            pl.BlockSpec((1, pairs, tile, PAIR), lambda m: (m // per, 0, m % per, 0)),
            pl.BlockSpec((pairs, tile, PAIR), lambda m: (0, jnp.maximum(m - first_tail, 0), 0)),
        ],
        out_shape=[
            jax.ShapeDtypeStruct((rows, head_width), BF),
            jax.ShapeDtypeStruct((blocks, pairs, UNIT, PAIR), BF),
            jax.ShapeDtypeStruct((pairs, UNIT, PAIR), BF),
        ],
        name="qkv",
    )(normed, weight, bias, *tables)


def fill_window(far, near, own, window, at):
    lanes = slice(at, at + LANES)
    window[0:UNIT] = far[0, :, lanes]
    for block in range(2):
        window[(1 + block) * UNIT : (2 + block) * UNIT] = near[block, 0, :, lanes]
        window[(3 + block) * UNIT : (4 + block) * UNIT] = own[block, 0, :, lanes]


def half_of(values, head):
    lane = lax.broadcasted_iota(jnp.int32, values.shape, 1)
    return jnp.where((lane >= HEAD_DIM) == bool(head), values, jnp.zeros_like(values))


def fwd_kernel(n_ref, q_ref, own_ref, near_ref, far_ref, o_ref, lse_ref, kw, vw, vt):
    fill_window(far_ref, near_ref, own_ref, kw, 0)
    fill_window(far_ref, near_ref, own_ref, vw, LANES)
    for block in range(5):
        rows = slice(block * UNIT, (block + 1) * UNIT)
        vt[:, rows] = vw[rows].T
    key_at = lax.broadcasted_iota(jnp.int32, (UNIT, UNIT), 0)
    query_at = lax.broadcasted_iota(jnp.int32, (UNIT, UNIT), 1)
    for block in range(2):
        rows = slice(block * UNIT, (block + 1) * UNIT)
        outs = []
        for head in range(2):
            query = half_of(q_ref[rows, :], head)
            part = slice(head * HEAD_DIM, (head + 1) * HEAD_DIM)
            at = (3 + block) * UNIT
            score = dot_nt(kw[at : at + UNIT], query)
            score = jnp.where(key_at <= query_at, score, MASKED)
            top = jnp.max(score, axis=0, keepdims=True)
            probs = jnp.exp(score - top)
            total = jnp.sum(probs, axis=0, keepdims=True)
            acc = dot_nn(vt[part, at : at + UNIT], probs.astype(BF))

            def step(back, carry, query=query, at=at, part=part):
                top, total, acc = carry
                where = pl.ds(pl.multiple_of(at - back * UNIT, UNIT), UNIT)
                score = dot_nt(kw[where], query)
                higher = jnp.maximum(top, jnp.max(score, axis=0, keepdims=True))
                shrink = jnp.exp(top - higher)
                probs = jnp.exp(score - higher)
                total = total * shrink + jnp.sum(probs, axis=0, keepdims=True)
                acc = acc * shrink + dot_nn(vt[part, where], probs.astype(BF))
                return higher, total, acc

            top, total, acc = lax.fori_loop(1, n_ref[block], step, (top, total, acc))
            outs.append(acc * (1.0 / total))
            lse_ref[0, head : head + 1, rows] = top + jnp.log(total)
        o_ref[rows, :] = jnp.concatenate(outs, axis=0).T.astype(BF)


def window_specs(rows, pairs):
    blocks = rows // UNIT
    kv_spec = pl.BlockSpec((blocks, 1, UNIT, PAIR), lambda p, n: (0, p, 0, 0))
    far_spec = pl.BlockSpec((1, UNIT, PAIR), lambda p, n: (p, 0, 0))
    row_spec = pl.BlockSpec((rows, LANES), lambda p, n: (0, p))
    return row_spec, kv_spec, far_spec


def fwd_call(counts, query, own, near, far):
    rows, head_width = query.shape
    pairs = head_width // LANES
    row_spec, kv_spec, far_spec = window_specs(rows, pairs)
    return pl.pallas_call(
        fwd_kernel,
        grid_spec=pltpu.PrefetchScalarGridSpec(
            num_scalar_prefetch=1,
            grid=(pairs,),
            in_specs=[row_spec, kv_spec, kv_spec, far_spec],
            out_specs=[row_spec, pl.BlockSpec((1, 2, rows), lambda p, n: (p, 0, 0))],
            scratch_shapes=[pltpu.VMEM((5 * UNIT, LANES), BF)] * 2
            + [pltpu.VMEM((LANES, 5 * UNIT), BF)],
        ),
        out_shape=[
            jax.ShapeDtypeStruct((rows, head_width), BF),
            jax.ShapeDtypeStruct((pairs, 2, rows), F32),
        ],
        name="attend",
    )(counts, query, own, near, far)


def bwd_kernel(
    n_ref, q_ref, own_ref, near_ref, far_ref, o_ref, do_ref, lse_ref, c_ref, s1_ref, s2_ref,
    dq_ref, down_ref, dnear_ref, dfar_ref, kw, vw, kt, dk, dv, dqt,
):
    fill_window(far_ref, near_ref, own_ref, kw, 0)
    fill_window(far_ref, near_ref, own_ref, vw, LANES)
    for block in range(5):
        rows = slice(block * UNIT, (block + 1) * UNIT)
        kt[:, rows] = kw[rows].T
    dk[...] = jnp.zeros_like(dk)
    dv[...] = jnp.zeros_like(dv)
    lane = lax.broadcasted_iota(jnp.int32, (UNIT, LANES), 1)
    key_at = lax.broadcasted_iota(jnp.int32, (UNIT, UNIT), 0)
    query_at = lax.broadcasted_iota(jnp.int32, (UNIT, UNIT), 1)
    for block in range(2):
        rows = slice(block * UNIT, (block + 1) * UNIT)
        grad = do_ref[rows, :]
        both = grad.astype(F32) * o_ref[rows, :].astype(F32)
        delta0 = jnp.sum(jnp.where(lane < HEAD_DIM, both, 0.0), axis=1, keepdims=True)
        delta1 = jnp.sum(jnp.where(lane < HEAD_DIM, 0.0, both), axis=1, keepdims=True)
        deltas = jnp.where(lane == 0, delta0, delta1).T
        dqt[...] = jnp.zeros_like(dqt)
        for head in range(2):
            query = half_of(q_ref[rows, :], head)
            grad_half = half_of(grad, head)
            lse = lse_ref[0, head : head + 1, rows]
            delta = deltas[head : head + 1, :]
            part = slice(head * HEAD_DIM, (head + 1) * HEAD_DIM)

            def visit(start, masked, query=query, grad_half=grad_half, lse=lse, delta=delta, part=part):
                where = pl.ds(start, UNIT)
                score = dot_nt(kw[where], query)
                if masked:
                    score = jnp.where(key_at <= query_at, score, MASKED)
                probs = jnp.exp(score - lse)
                probs_grad = dot_nt(vw[where], grad_half)
                score_grad = (probs * (probs_grad - delta)).astype(BF)
                dv[where] += dot_nn(probs.astype(BF), grad_half)
                dk[where] += dot_nn(score_grad, query)
                dqt[part, :] += dot_nn(kt[part, where], score_grad)

            at = (3 + block) * UNIT
            visit(at, True)

            def step(back, carry, at=at, visit=visit):
                visit(pl.multiple_of(at - back * UNIT, UNIT), False)
                return carry

            lax.fori_loop(1, n_ref[block], step, 0)
        dq = dqt[...].T * HEAD_DIM**-0.5
        dq_ref[rows, :] = turned_back(dq, c_ref[rows, :], s1_ref[rows, :], s2_ref[rows, :]).astype(BF)
    for source, at in ((dk, 0), (dv, LANES)):
        lanes = slice(at, at + LANES)
        dfar_ref[0, :, lanes] = source[0:UNIT].astype(BF)
        for block in range(2):
            dnear_ref[block, 0, :, lanes] = source[(1 + block) * UNIT : (2 + block) * UNIT].astype(BF)
            down_ref[block, 0, :, lanes] = source[(3 + block) * UNIT : (4 + block) * UNIT]


def bwd_call(counts, query, own, near, far, out, out_grad, lse, tables):
    rows, head_width = query.shape
    pairs = head_width // LANES
    blocks = rows // UNIT
    row_spec, kv_spec, far_spec = window_specs(rows, pairs)
    table_spec = pl.BlockSpec((rows, LANES), lambda p, n: (0, 0))
    return pl.pallas_call(
        bwd_kernel,
        grid_spec=pltpu.PrefetchScalarGridSpec(
            num_scalar_prefetch=1,
            grid=(pairs,),
            in_specs=[row_spec, kv_spec, kv_spec, far_spec, row_spec, row_spec]
            + [pl.BlockSpec((1, 2, rows), lambda p, n: (p, 0, 0))]
            + [table_spec] * 3,
            out_specs=[row_spec, kv_spec, kv_spec, far_spec],
            scratch_shapes=[pltpu.VMEM((5 * UNIT, LANES), BF)] * 2
            + [pltpu.VMEM((LANES, 5 * UNIT), BF)]
            + [pltpu.VMEM((5 * UNIT, LANES), F32)] * 2
            + [pltpu.VMEM((LANES, UNIT), F32)],
        ),
        out_shape=[
            jax.ShapeDtypeStruct((rows, head_width), BF),
            jax.ShapeDtypeStruct((blocks, pairs, UNIT, PAIR), F32),
            jax.ShapeDtypeStruct((blocks, pairs, UNIT, PAIR), BF),
            jax.ShapeDtypeStruct((pairs, UNIT, PAIR), BF),
        ],
        name="attend_back",
    )(counts, query, own, near, far, out, out_grad, lse, *tables)


def join_kernel(dq_ref, own_ref, near_ref, far_ref, c_ref, s1_ref, s2_ref, jg_ref, sum_ref):
    block = pl.program_id(0)
    cosine, low, high = c_ref[...], s1_ref[...], s2_ref[...]
    pairs = dq_ref.shape[1] // LANES
    last = (block == pl.num_programs(0) - 1).astype(F32)
    parts = [dq_ref[:, p * LANES : (p + 1) * LANES] for p in range(pairs)]
    for at in (0, LANES):
        for pair in range(pairs):
            lanes = slice(at, at + LANES)
            grad = own_ref[0, pair, :, lanes] + near_ref[0, pair, :, lanes].astype(F32)
            grad = grad + last * far_ref[pair, :, lanes].astype(F32)
            if at == 0:
                grad = turned_back(grad, cosine, low, high)
            parts.append(grad.astype(BF))
    for index, part in enumerate(parts):
        lanes = slice(index * LANES, (index + 1) * LANES)
        jg_ref[:, lanes] = part
        column = jnp.sum(part.astype(F32), axis=0, keepdims=True)

        @pl.when(block == 0)
        def _():
            sum_ref[:, lanes] = column

        @pl.when(block > 0)
        def _():
            sum_ref[:, lanes] += column


def join_call(dq, own, near, far, tables):
    rows, head_width = dq.shape
    pairs = head_width // LANES
    blocks = rows // UNIT
    table_spec = pl.BlockSpec((UNIT, LANES), lambda b: (b, 0))
    kv_spec = pl.BlockSpec((1, pairs, UNIT, PAIR), lambda b: (b, 0, 0, 0))
    return pl.pallas_call(
        join_kernel,
        grid=(blocks,),
        in_specs=[
            pl.BlockSpec((UNIT, head_width), lambda b: (b, 0)),
            kv_spec,
            kv_spec,
            pl.BlockSpec((pairs, UNIT, PAIR), lambda b: (0, 0, 0)),
        ]
        + [table_spec] * 3,
        out_specs=[
            pl.BlockSpec((UNIT, 3 * head_width), lambda b: (b, 0)),
            pl.BlockSpec((1, 3 * head_width), lambda b: (0, 0)),
        ],
        out_shape=[
            jax.ShapeDtypeStruct((rows, 3 * head_width), BF),
            jax.ShapeDtypeStruct((1, 3 * head_width), F32),
        ],
        name="join",
    )(dq, own, near, far, *tables)


def up_kernel(x_ref, w_ref, b_ref, hidden_ref, slope_ref):
    rise = dot_nn(x_ref[...], w_ref[...]) + b_ref[...]
    phi = 0.5 + 0.5 * lax.erf(rise * 0.7071067811865476)
    bell = jnp.exp(rise * rise * -0.5) * 0.3989422804014327
    hidden_ref[...] = (rise * phi).astype(BF)
    slope_ref[...] = phi + rise * bell


def up_call(normed, weight, bias):
    rows, width = normed.shape
    cols = weight.shape[1]
    tile = 256
    return pl.pallas_call(
        up_kernel,
        grid=(rows // tile,),
        in_specs=[
            pl.BlockSpec((tile, width), lambda m: (m, 0)),
            pl.BlockSpec((width, cols), lambda m: (0, 0)),
            pl.BlockSpec((1, cols), lambda m: (0, 0)),
        ],
        out_specs=[pl.BlockSpec((tile, cols), lambda m: (m, 0))] * 2,
        out_shape=[
            jax.ShapeDtypeStruct((rows, cols), BF),
            jax.ShapeDtypeStruct((rows, cols), F32),
        ],
        name="up",
    )(normed, weight, bias)


def grad_kernel(side_ref, left_ref, *refs, chunk):
    rights, mine_ref, sent_ref = refs[:-2], refs[-2], refs[-1]
    first = side_ref[0] == 0
    at = 0
    for right_ref in rights:
        cols = slice(at, at + right_ref.shape[1])
        at += right_ref.shape[1]
        product = dot_tn(left_ref[...], right_ref[...])
        for pair in range(product.shape[0] // (2 * chunk)):
            low = product[2 * pair * chunk : (2 * pair + 1) * chunk]
            high = product[(2 * pair + 1) * chunk : (2 * pair + 2) * chunk]
            mine_ref[pair, :, cols] = jnp.where(first, low, high).astype(mine_ref.dtype)
            sent_ref[pair, :, cols] = jnp.where(first, high, low).astype(BF)


def grad_call(side, left, rights, chunk):
    rows, width = left.shape
    cols = sum(right.shape[1] for right in rights)
    tile = max(256, 2 * chunk)
    pairs = tile // (2 * chunk)
    outer = width // (2 * chunk)
    out_spec = pl.BlockSpec((pairs, chunk, cols), lambda m, s: (m, 0, 0))
    return pl.pallas_call(
        functools.partial(grad_kernel, chunk=chunk),
        grid_spec=pltpu.PrefetchScalarGridSpec(
            num_scalar_prefetch=1,
            grid=(width // tile,),
            in_specs=[pl.BlockSpec((rows, tile), lambda m, s: (0, m))]
            + [pl.BlockSpec(right.shape, lambda m, s: (0, 0)) for right in rights],
            out_specs=[out_spec, out_spec],
        ),
        out_shape=[
            jax.ShapeDtypeStruct((outer, chunk, cols), BF),
            jax.ShapeDtypeStruct((outer, chunk, cols), BF),
        ],
        name="weight_grad",
    )(side, left, *rights)


def pair_kernel(at_ref, mine_ref, came_ref, own_ref, *part_refs):
    turn = pl.program_id(0)
    total = mine_ref[0].astype(F32) + came_ref[0].astype(F32)

    @pl.when(turn == 0)
    def _():
        own_ref[...] = total

    for index, part_ref in enumerate(part_refs):

        @pl.when(turn == index + 1)
        def _(part_ref=part_ref):
            part_ref[...] = total.astype(BF)


def pair_call(at, mine, came):
    outer, chunk, cols = mine.shape
    in_spec = pl.BlockSpec((1, chunk, cols), lambda d, a: ((a[0] + d) % outer, 0, 0))
    out_spec = pl.BlockSpec((chunk, cols), lambda d, a: (0, 0))
    return pl.pallas_call(
        pair_kernel,
        grid_spec=pltpu.PrefetchScalarGridSpec(
            num_scalar_prefetch=1,
            grid=(outer,),
            in_specs=[in_spec, in_spec],
            out_specs=[out_spec] * outer,
        ),
        out_shape=[jax.ShapeDtypeStruct((chunk, cols), F32)]
        + [jax.ShapeDtypeStruct((chunk, cols), BF)] * (outer - 1),
        name="pair_sum",
    )(at, mine, came)


def place_kernel(me_ref, own_ref, beside_ref, across_ref, diagonal_ref, out_ref):
    for index, ref in enumerate((own_ref, beside_ref, across_ref, diagonal_ref)):

        @pl.when(pl.program_id(0) == index)
        def _(ref=ref):
            out_ref[...] = ref[...]


def place_call(me, blocks):
    rows, width = blocks[0].shape
    whole = pl.BlockSpec((rows, width), lambda i, m: (0, 0))
    return pl.pallas_call(
        place_kernel,
        grid_spec=pltpu.PrefetchScalarGridSpec(
            num_scalar_prefetch=1,
            grid=(4,),
            in_specs=[whole] * 4,
            out_specs=pl.BlockSpec((rows, width), lambda i, m: (m[0] ^ i, 0)),
        ),
        out_shape=jax.ShapeDtypeStruct((4 * rows, width), blocks[0].dtype),
        name="place",
    )(me, *blocks)


def flipped(count, bit):
    return [(i, i ^ bit) for i in range(count)]


def shifted(count, distance):
    devices = range(count)
    return [(i - distance, i) for i in devices if i - distance in devices]


def rolled_outer(outer, distance):
    return [
        (o * 2 + y, (o + distance) % outer * 2 + y) for o in range(outer) for y in range(2)
    ]


def gather_rows(piece):
    count = lax.axis_size("seq")
    outer = count // 2
    place = lax.axis_index("seq")
    at, side = place // 2, place % 2
    chunk, cols = piece.shape
    line = jnp.zeros((outer, chunk, cols), piece.dtype)
    line = lax.dynamic_update_index_in_dim(line, piece, at, 0)
    for distance in range(1, outer):
        came = lax.ppermute(piece, "seq", rolled_outer(outer, distance))
        line = lax.dynamic_update_index_in_dim(line, came, (at - distance) % outer, 0)
    other = lax.ppermute(line, "seq", flipped(count, 1))
    full = jnp.zeros((outer, 2, chunk, cols), piece.dtype)
    full = lax.dynamic_update_index_in_dim(full, line, side, 1)
    full = lax.dynamic_update_index_in_dim(full, other, 1 - side, 1)
    return full.reshape(count * chunk, cols)


def gather_rows_whole(piece):
    return lax.all_gather(piece, "seq", axis=0, tiled=True)


def scatter_grad(left, rights):
    count = lax.axis_size("seq")
    outer = count // 2
    place = lax.axis_index("seq")
    chunk = left.shape[1] // count
    mine, sent = grad_call((place % 2)[None], left, rights, chunk)
    came = lax.ppermute(sent, "seq", flipped(count, 1))
    total, *parts = pair_call((place // 2)[None], mine, came)
    for distance, part in enumerate(parts, 1):
        total = total + lax.ppermute(part, "seq", rolled_outer(outer, distance)).astype(F32)
    return total


def gather_tokens(rows):
    count = lax.axis_size("tensor")
    me = lax.axis_index("tensor")
    across = lax.ppermute(rows, "tensor", flipped(count, 2))
    beside = lax.ppermute(rows, "tensor", flipped(count, 1))
    diagonal = lax.ppermute(across, "tensor", flipped(count, 1))
    return place_call(me[None], (rows, beside, across, diagonal))


def scatter_tokens(partial):
    count = lax.axis_size("tensor")
    me = lax.axis_index("tensor")
    core, chip = me % 2, me // 2
    split = partial.reshape(2, 2, partial.shape[0] // count, partial.shape[1])
    sent = lax.dynamic_index_in_dim(split, 1 - core, 1, keepdims=False)
    kept = lax.dynamic_index_in_dim(split, core, 1, keepdims=False)
    came = lax.ppermute(sent, "tensor", flipped(count, 1))
    far = lax.dynamic_index_in_dim(kept, 1 - chip, 0, keepdims=False).astype(F32)
    far = far + lax.dynamic_index_in_dim(came, 1 - chip, 0, keepdims=False).astype(F32)
    across = lax.ppermute(far.astype(BF), "tensor", flipped(count, 2))
    near = lax.dynamic_index_in_dim(kept, chip, 0, keepdims=False).astype(F32)
    near = near + lax.dynamic_index_in_dim(came, chip, 0, keepdims=False).astype(F32)
    return near + across.astype(F32)


def exchanged(rows):
    return lax.all_to_all(rows, ("seq", "tensor"), 0, 0, tiled=True)


def layer_norm(values, gain, shift):
    center = values - jnp.mean(values, axis=1, keepdims=True)
    scale_inv = lax.rsqrt(jnp.mean(center * center, axis=1, keepdims=True) + EPSILON)
    unit = center * scale_inv
    return (unit * gain + shift, unit, scale_inv)


def norm_back(grad, unit, scale_inv, gain):
    scaled = grad * gain
    return scale_inv * (
        scaled
        - jnp.mean(scaled, axis=1, keepdims=True)
        - unit * jnp.mean(scaled * unit, axis=1, keepdims=True)
    )


def rotary_tables(offsets):
    exponent = jnp.arange(0, ROT, 2).astype(F32) / ROT
    rates = 10000.0 ** (-exponent)
    head = jnp.concatenate([rates, rates, jnp.zeros(HEAD_DIM - ROT, F32)])
    lane = jnp.arange(LANES) % HEAD_DIM
    angles = offsets.astype(F32)[:, None] * jnp.concatenate([head, head])[None, :]
    sine = jnp.sin(angles)
    low = jnp.where(lane < ROT // 2, -sine, 0.0)
    high = jnp.where((lane >= ROT // 2) & (lane < ROT), sine, 0.0)
    return (jnp.cos(angles), low, high)


def local(
    block_input,
    lengths,
    ln_gain,
    ln_bias,
    qkv_weight,
    qkv_bias,
    out_weight,
    up_weight,
    up_bias,
    down_weight,
    out_bias,
    out_grad,
):
    tensor_count = lax.axis_size("tensor")
    seq_count = lax.axis_size("seq")
    everyone = seq_count * tensor_count
    me_tensor = lax.axis_index("tensor")
    own_rows, width = block_input.shape
    group = own_rows * tensor_count
    layers = qkv_weight.shape[0]
    chunk = qkv_weight.shape[1]
    head_width = qkv_weight.shape[3]
    heads = head_width // HEAD_DIM
    hidden_width = up_weight.shape[2]
    first = lax.axis_index("seq") * group
    positions = first + jnp.arange(group, dtype=jnp.int32)
    ends = jnp.cumsum(lengths)
    starts_of = jnp.sum(jnp.where(ends[None, :] <= positions[:, None], lengths[None, :], 0), axis=1)
    offsets = positions - starts_of
    tables = rotary_tables(offsets)
    counts = offsets[::UNIT] // UNIT + 1

    small_sizes = []
    pieces = []
    for array in (ln_gain, ln_bias, out_bias, qkv_bias, up_bias):
        pieces.append(array.reshape(-1))
        small_sizes.append(array.size)
    packed = jnp.concatenate(pieces)
    small = exchanged(jnp.broadcast_to(packed[None, :], (everyone, packed.size)))
    parts = []
    at = 0
    for size in small_sizes:
        parts.append(small[:, at : at + size])
        at += size

    def over_all(part):
        return jnp.transpose(part.reshape(everyone, layers, -1), (1, 0, 2)).reshape(layers, width)

    def over_seq(part):
        part = part.reshape(seq_count, tensor_count, -1)
        return lax.dynamic_index_in_dim(part, me_tensor, 1, keepdims=False)

    gains = over_all(parts[0]).astype(F32)
    shifts = over_all(parts[1]).astype(F32)
    out_biases = over_all(parts[2]).astype(F32)
    per = HEAD_DIM // seq_count
    joint_bias = over_seq(parts[3]).reshape(seq_count, layers, 3, heads, per)
    joint_bias = jnp.transpose(joint_bias, (1, 2, 3, 0, 4)).reshape(layers, 1, 3 * head_width)
    joint_bias = joint_bias.astype(F32)
    groups = up_bias.shape[1]
    rise_bias = over_seq(parts[4]).reshape(seq_count, layers, groups, -1)
    rise_bias = jnp.transpose(rise_bias, (1, 2, 0, 3)).reshape(layers, 1, hidden_width).astype(F32)

    weights = []
    for layer in range(layers):
        gather = GATHER[layer]
        weights.append(
            (
                gather(qkv_weight[layer].reshape(chunk, 3 * head_width)),
                gather(up_weight[layer]),
                gather(jnp.concatenate([out_weight[layer], down_weight[layer]], axis=1)),
            )
        )

    kept = []
    current = block_input
    for layer in range(layers):
        qkv_full, up_full, fall_full = weights[layer]
        normed, unit, scale_inv = layer_norm(current, gains[layer][None], shifts[layer][None])
        normed_rows = gather_tokens(normed.astype(BF))
        query, own, tail = qkv_call(normed_rows, qkv_full, joint_bias[layer], tables)
        near = lax.ppermute(own, "seq", shifted(seq_count, 1))
        far = lax.ppermute(tail, "seq", shifted(seq_count, 2))
        hidden, slope = up_call(normed_rows, up_full, rise_bias[layer])
        mixed, lse = fwd_call(counts, query, own, near, far)
        partial = dot_nt(mixed, fall_full[:, :head_width]) + dot_nt(hidden, fall_full[:, head_width:])
        branch = scatter_tokens(partial.astype(BF))
        kept.append((normed_rows, unit, scale_inv, query, own, near, far, hidden, slope, mixed, lse))
        current = current + branch + out_biases[layer][None, :]

    gradient = out_grad
    collected = []
    for layer in reversed(range(layers)):
        qkv_full, up_full, fall_full = weights[layer]
        normed_rows, unit, scale_inv, query, own, near, far, hidden, slope, mixed, lse = kept[layer]
        bias_grad = jnp.sum(gradient, axis=0)
        grad_rows = gather_tokens(gradient.astype(BF))
        mixed_grad = dot_nn(grad_rows, fall_full[:, :head_width]).astype(BF)
        whole = WHOLE[layer]
        if not whole:
            fall_grad = scatter_grad(grad_rows, (mixed, hidden))
        dq, down, dnear, dfar = bwd_call(counts, query, own, near, far, mixed, mixed_grad, lse, tables)
        came_near = lax.ppermute(dnear, "seq", shifted(seq_count, -1))
        came_far = lax.ppermute(dfar, "seq", shifted(seq_count, -2))
        hidden_grad = dot_nn(grad_rows, fall_full[:, head_width:])
        rise_grad = (hidden_grad * slope).astype(BF)
        rise_bias_grad = jnp.sum(rise_grad, axis=0, dtype=F32)
        if not whole:
            up_grad = scatter_grad(normed_rows, (rise_grad,))
        normed_part = dot_nt(rise_grad, up_full)
        joint_grad, joint_bias_grad = join_call(dq, down, came_near, came_far, tables)
        if whole:
            every = jnp.concatenate(
                [
                    dot_tn(grad_rows, jnp.concatenate([mixed, hidden], axis=1)).astype(BF),
                    dot_tn(normed_rows, rise_grad).astype(BF),
                    dot_tn(normed_rows, joint_grad).astype(BF),
                ],
                axis=1,
            )
            every = lax.psum_scatter(every, "seq", scatter_dimension=0, tiled=True).astype(F32)
            fall_grad = every[:, : head_width + hidden_width]
            up_grad = every[:, head_width + hidden_width : head_width + 2 * hidden_width]
            joint_weight_grad = every[:, head_width + 2 * hidden_width :]
        else:
            joint_weight_grad = scatter_grad(normed_rows, (joint_grad,))
        normed_part = normed_part + dot_nt(joint_grad, qkv_full)
        normed_grad = scatter_tokens(normed_part.astype(BF))
        gain_grad = jnp.sum(normed_grad * unit, axis=0)
        shift_grad = jnp.sum(normed_grad, axis=0)
        gradient = gradient + norm_back(normed_grad, unit, scale_inv, gains[layer][None, :])
        collected.append(
            (gain_grad, shift_grad, bias_grad, joint_bias_grad.reshape(-1), rise_bias_grad,
             joint_weight_grad, fall_grad, up_grad)
        )
    collected = collected[::-1]

    def stacked(member):
        return jnp.stack([entry[member] for entry in collected])

    def to_all(member):
        value = stacked(member).reshape(layers, everyone, -1)
        return jnp.transpose(value, (1, 0, 2)).reshape(everyone, -1)

    def to_seq(value):
        mine = jnp.arange(tensor_count)[None, :, None] == me_tensor
        return jnp.where(mine, value[:, None, :], 0.0).reshape(everyone, -1)

    joint_out = stacked(3).reshape(layers, 3, heads, seq_count, per)
    joint_out = jnp.transpose(joint_out, (3, 0, 1, 2, 4)).reshape(seq_count, -1)
    rise_out = stacked(4).reshape(layers, groups, seq_count, -1)
    rise_out = jnp.transpose(rise_out, (2, 0, 1, 3)).reshape(seq_count, -1)
    outgoing = jnp.concatenate(
        [to_all(0), to_all(1), to_all(2), to_seq(joint_out), to_seq(rise_out)], axis=1
    )
    summed = jnp.sum(exchanged(outgoing), axis=0)
    results = []
    at = 0
    for array in (ln_gain, ln_bias, out_bias, qkv_bias, up_bias):
        results.append(summed[at : at + array.size].reshape(array.shape))
        at += array.size
    joint_weight_grad = stacked(5).reshape(layers, chunk, 3, head_width)
    fall_grad = stacked(6)
    return (
        current,
        gradient,
        results[0],
        results[1],
        joint_weight_grad,
        results[3],
        fall_grad[:, :, :head_width],
        stacked(7),
        results[4],
        fall_grad[:, :, head_width:],
        results[2],
    )


GATHER = (gather_rows, gather_rows_whole)
WHOLE = (False, True)


def solution(mesh):
    tokens = P(("seq", "tensor"), None)
    vector = P(None, ("seq", "tensor"))
    matrix = P(None, "seq", "tensor")
    joint = P(None, "seq", None, "tensor")
    joint_vector = P(None, None, "tensor", "seq")
    rise_vector = P(None, "tensor", "seq")
    in_specs = (
        tokens, P(), vector, vector, joint, joint_vector, matrix, matrix, rise_vector, matrix,
        vector, tokens,
    )
    out_specs = (
        tokens, tokens, vector, vector, joint, joint_vector, matrix, matrix, rise_vector, matrix,
        vector,
    )
    return jax.shard_map(local, mesh=mesh, in_specs=in_specs, out_specs=out_specs, check_vma=False)
```

```python
import functools
import jax
import jax.numpy as jnp
from jax import lax
from jax.experimental import pallas as pl
from jax.experimental.pallas import tpu as pltpu
from jax.sharding import PartitionSpec as P

HEAD_DIM = 64
ROT = 16
UNIT = 512
LANES = 128
PAIR = 2 * LANES
EPSILON = 1e-05
MASKED = -1e30
BF = jnp.bfloat16
F32 = jnp.float32


def dot_nn(left, right):
    return lax.dot_general(left, right, (((1,), (0,)), ((), ())), preferred_element_type=F32)


def dot_nt(left, right):
    return lax.dot_general(left, right, (((1,), (1,)), ((), ())), preferred_element_type=F32)


def dot_tn(left, right):
    return lax.dot_general(left, right, (((0,), (0,)), ((), ())), preferred_element_type=F32)


def turned(values, cosine, sine_low, sine_high):
    ahead = pltpu.roll(values, LANES - ROT // 2, 1)
    behind = pltpu.roll(values, ROT // 2, 1)
    return values * cosine + ahead * sine_low + behind * sine_high


def turned_back(grad, cosine, sine_low, sine_high):
    ahead = pltpu.roll(grad, LANES - ROT // 2, 1)
    behind = pltpu.roll(grad, ROT // 2, 1)
    return grad * cosine - ahead * sine_low - behind * sine_high


def qkv_kernel(x_ref, w_ref, b_ref, c_ref, s1_ref, s2_ref, q_ref, kv_ref, tail_ref):
    joint = dot_nn(x_ref[...], w_ref[...]) + b_ref[...]
    cosine, low, high = c_ref[...], s1_ref[...], s2_ref[...]
    pairs = q_ref.shape[1] // LANES
    for pair in range(pairs):
        lanes = slice(pair * LANES, (pair + 1) * LANES)
        query = turned(joint[:, lanes], cosine, low, high) * HEAD_DIM**-0.5
        q_ref[:, lanes] = query.astype(BF)
        at = (pairs + pair) * LANES
        key = turned(joint[:, at : at + LANES], cosine, low, high).astype(BF)
        at = (2 * pairs + pair) * LANES
        value = joint[:, at : at + LANES].astype(BF)
        kv_ref[0, pair, :, :LANES] = key
        kv_ref[0, pair, :, LANES:] = value
        tail_ref[pair, :, :LANES] = key
        tail_ref[pair, :, LANES:] = value


def qkv_call(normed, weight, bias, tables):
    rows, width = normed.shape
    cols = weight.shape[1]
    head_width = cols // 3
    pairs = head_width // LANES
    blocks = rows // UNIT
    tile = 256
    per = UNIT // tile
    row_spec = pl.BlockSpec((tile, LANES), lambda m: (m, 0))
    first_tail = (blocks - 1) * per
    return pl.pallas_call(
        qkv_kernel,
        grid=(rows // tile,),
        in_specs=[
            pl.BlockSpec((tile, width), lambda m: (m, 0)),
            pl.BlockSpec((width, cols), lambda m: (0, 0)),
            pl.BlockSpec((1, cols), lambda m: (0, 0)),
            row_spec,
            row_spec,
            row_spec,
        ],
        out_specs=[
            pl.BlockSpec((tile, head_width), lambda m: (m, 0)),
            pl.BlockSpec((1, pairs, tile, PAIR), lambda m: (m // per, 0, m % per, 0)),
            pl.BlockSpec((pairs, tile, PAIR), lambda m: (0, jnp.maximum(m - first_tail, 0), 0)),
        ],
        out_shape=[
            jax.ShapeDtypeStruct((rows, head_width), BF),
            jax.ShapeDtypeStruct((blocks, pairs, UNIT, PAIR), BF),
            jax.ShapeDtypeStruct((pairs, UNIT, PAIR), BF),
        ],
        name="qkv",
    )(normed, weight, bias, *tables)


def fill_window(far, near, own, window, at):
    lanes = slice(at, at + LANES)
    window[0:UNIT] = far[0, :, lanes]
    for block in range(2):
        window[(1 + block) * UNIT : (2 + block) * UNIT] = near[block, 0, :, lanes]
        window[(3 + block) * UNIT : (4 + block) * UNIT] = own[block, 0, :, lanes]


def half_of(values, head):
    lane = lax.broadcasted_iota(jnp.int32, values.shape, 1)
    return jnp.where((lane >= HEAD_DIM) == bool(head), values, jnp.zeros_like(values))


def fwd_kernel(n_ref, q_ref, own_ref, near_ref, far_ref, o_ref, lse_ref, kw, vw, vt):
    fill_window(far_ref, near_ref, own_ref, kw, 0)
    fill_window(far_ref, near_ref, own_ref, vw, LANES)
    for block in range(5):
        rows = slice(block * UNIT, (block + 1) * UNIT)
        vt[:, rows] = vw[rows].T
    key_at = lax.broadcasted_iota(jnp.int32, (UNIT, UNIT), 0)
    query_at = lax.broadcasted_iota(jnp.int32, (UNIT, UNIT), 1)
    for block in range(2):
        rows = slice(block * UNIT, (block + 1) * UNIT)
        outs = []
        for head in range(2):
            query = half_of(q_ref[rows, :], head)
            part = slice(head * HEAD_DIM, (head + 1) * HEAD_DIM)
            at = (3 + block) * UNIT
            score = dot_nt(kw[at : at + UNIT], query)
            score = jnp.where(key_at <= query_at, score, MASKED)
            top = jnp.max(score, axis=0, keepdims=True)
            probs = jnp.exp(score - top)
            total = jnp.sum(probs, axis=0, keepdims=True)
            acc = dot_nn(vt[part, at : at + UNIT], probs.astype(BF))

            def step(back, carry, query=query, at=at, part=part):
                top, total, acc = carry
                where = pl.ds(pl.multiple_of(at - back * UNIT, UNIT), UNIT)
                score = dot_nt(kw[where], query)
                higher = jnp.maximum(top, jnp.max(score, axis=0, keepdims=True))
                shrink = jnp.exp(top - higher)
                probs = jnp.exp(score - higher)
                total = total * shrink + jnp.sum(probs, axis=0, keepdims=True)
                acc = acc * shrink + dot_nn(vt[part, where], probs.astype(BF))
                return higher, total, acc

            top, total, acc = lax.fori_loop(1, n_ref[block], step, (top, total, acc))
            outs.append(acc * (1.0 / total))
            lse_ref[0, head : head + 1, rows] = top + jnp.log(total)
        o_ref[rows, :] = jnp.concatenate(outs, axis=0).T.astype(BF)


def window_specs(rows, pairs):
    blocks = rows // UNIT
    kv_spec = pl.BlockSpec((blocks, 1, UNIT, PAIR), lambda p, n: (0, p, 0, 0))
    far_spec = pl.BlockSpec((1, UNIT, PAIR), lambda p, n: (p, 0, 0))
    row_spec = pl.BlockSpec((rows, LANES), lambda p, n: (0, p))
    return row_spec, kv_spec, far_spec


def fwd_call(counts, query, own, near, far):
    rows, head_width = query.shape
    pairs = head_width // LANES
    row_spec, kv_spec, far_spec = window_specs(rows, pairs)
    return pl.pallas_call(
        fwd_kernel,
        grid_spec=pltpu.PrefetchScalarGridSpec(
            num_scalar_prefetch=1,
            grid=(pairs,),
            in_specs=[row_spec, kv_spec, kv_spec, far_spec],
            out_specs=[row_spec, pl.BlockSpec((1, 2, rows), lambda p, n: (p, 0, 0))],
            scratch_shapes=[pltpu.VMEM((5 * UNIT, LANES), BF)] * 2
            + [pltpu.VMEM((LANES, 5 * UNIT), BF)],
        ),
        out_shape=[
            jax.ShapeDtypeStruct((rows, head_width), BF),
            jax.ShapeDtypeStruct((pairs, 2, rows), F32),
        ],
        name="attend",
    )(counts, query, own, near, far)


def bwd_kernel(
    n_ref, q_ref, own_ref, near_ref, far_ref, o_ref, do_ref, lse_ref, c_ref, s1_ref, s2_ref,
    dq_ref, down_ref, dnear_ref, dfar_ref, kw, vw, kt, dk, dv, dqt,
):
    fill_window(far_ref, near_ref, own_ref, kw, 0)
    fill_window(far_ref, near_ref, own_ref, vw, LANES)
    for block in range(5):
        rows = slice(block * UNIT, (block + 1) * UNIT)
        kt[:, rows] = kw[rows].T
    dk[...] = jnp.zeros_like(dk)
    dv[...] = jnp.zeros_like(dv)
    lane = lax.broadcasted_iota(jnp.int32, (UNIT, LANES), 1)
    key_at = lax.broadcasted_iota(jnp.int32, (UNIT, UNIT), 0)
    query_at = lax.broadcasted_iota(jnp.int32, (UNIT, UNIT), 1)
    for block in range(2):
        rows = slice(block * UNIT, (block + 1) * UNIT)
        grad = do_ref[rows, :]
        both = grad.astype(F32) * o_ref[rows, :].astype(F32)
        delta0 = jnp.sum(jnp.where(lane < HEAD_DIM, both, 0.0), axis=1, keepdims=True)
        delta1 = jnp.sum(jnp.where(lane < HEAD_DIM, 0.0, both), axis=1, keepdims=True)
        deltas = jnp.where(lane == 0, delta0, delta1).T
        dqt[...] = jnp.zeros_like(dqt)
        for head in range(2):
            query = half_of(q_ref[rows, :], head)
            grad_half = half_of(grad, head)
            lse = lse_ref[0, head : head + 1, rows]
            delta = deltas[head : head + 1, :]
            part = slice(head * HEAD_DIM, (head + 1) * HEAD_DIM)

            def visit(start, masked, query=query, grad_half=grad_half, lse=lse, delta=delta, part=part):
                where = pl.ds(start, UNIT)
                score = dot_nt(kw[where], query)
                if masked:
                    score = jnp.where(key_at <= query_at, score, MASKED)
                probs = jnp.exp(score - lse)
                probs_grad = dot_nt(vw[where], grad_half)
                score_grad = (probs * (probs_grad - delta)).astype(BF)
                dv[where] += dot_nn(probs.astype(BF), grad_half)
                dk[where] += dot_nn(score_grad, query)
                dqt[part, :] += dot_nn(kt[part, where], score_grad)

            at = (3 + block) * UNIT
            visit(at, True)

            def step(back, carry, at=at, visit=visit):
                visit(pl.multiple_of(at - back * UNIT, UNIT), False)
                return carry

            lax.fori_loop(1, n_ref[block], step, 0)
        dq = dqt[...].T * HEAD_DIM**-0.5
        dq_ref[rows, :] = turned_back(dq, c_ref[rows, :], s1_ref[rows, :], s2_ref[rows, :]).astype(BF)
    for source, at in ((dk, 0), (dv, LANES)):
        lanes = slice(at, at + LANES)
        dfar_ref[0, :, lanes] = source[0:UNIT].astype(BF)
        for block in range(2):
            dnear_ref[block, 0, :, lanes] = source[(1 + block) * UNIT : (2 + block) * UNIT].astype(BF)
            down_ref[block, 0, :, lanes] = source[(3 + block) * UNIT : (4 + block) * UNIT]


def bwd_call(counts, query, own, near, far, out, out_grad, lse, tables):
    rows, head_width = query.shape
    pairs = head_width // LANES
    blocks = rows // UNIT
    row_spec, kv_spec, far_spec = window_specs(rows, pairs)
    table_spec = pl.BlockSpec((rows, LANES), lambda p, n: (0, 0))
    return pl.pallas_call(
        bwd_kernel,
        grid_spec=pltpu.PrefetchScalarGridSpec(
            num_scalar_prefetch=1,
            grid=(pairs,),
            in_specs=[row_spec, kv_spec, kv_spec, far_spec, row_spec, row_spec]
            + [pl.BlockSpec((1, 2, rows), lambda p, n: (p, 0, 0))]
            + [table_spec] * 3,
            out_specs=[row_spec, kv_spec, kv_spec, far_spec],
            scratch_shapes=[pltpu.VMEM((5 * UNIT, LANES), BF)] * 2
            + [pltpu.VMEM((LANES, 5 * UNIT), BF)]
            + [pltpu.VMEM((5 * UNIT, LANES), F32)] * 2
            + [pltpu.VMEM((LANES, UNIT), F32)],
        ),
        out_shape=[
            jax.ShapeDtypeStruct((rows, head_width), BF),
            jax.ShapeDtypeStruct((blocks, pairs, UNIT, PAIR), F32),
            jax.ShapeDtypeStruct((blocks, pairs, UNIT, PAIR), BF),
            jax.ShapeDtypeStruct((pairs, UNIT, PAIR), BF),
        ],
        name="attend_back",
    )(counts, query, own, near, far, out, out_grad, lse, *tables)


def join_kernel(dq_ref, own_ref, near_ref, far_ref, c_ref, s1_ref, s2_ref, jg_ref, sum_ref):
    block = pl.program_id(0)
    cosine, low, high = c_ref[...], s1_ref[...], s2_ref[...]
    pairs = dq_ref.shape[1] // LANES
    last = (block == pl.num_programs(0) - 1).astype(F32)
    parts = [dq_ref[:, p * LANES : (p + 1) * LANES] for p in range(pairs)]
    for at in (0, LANES):
        for pair in range(pairs):
            lanes = slice(at, at + LANES)
            grad = own_ref[0, pair, :, lanes] + near_ref[0, pair, :, lanes].astype(F32)
            grad = grad + last * far_ref[pair, :, lanes].astype(F32)
            if at == 0:
                grad = turned_back(grad, cosine, low, high)
            parts.append(grad.astype(BF))
    for index, part in enumerate(parts):
        lanes = slice(index * LANES, (index + 1) * LANES)
        jg_ref[:, lanes] = part
        column = jnp.sum(part.astype(F32), axis=0, keepdims=True)

        @pl.when(block == 0)
        def _():
            sum_ref[:, lanes] = column

        @pl.when(block > 0)
        def _():
            sum_ref[:, lanes] += column


def join_call(dq, own, near, far, tables):
    rows, head_width = dq.shape
    pairs = head_width // LANES
    blocks = rows // UNIT
    table_spec = pl.BlockSpec((UNIT, LANES), lambda b: (b, 0))
    kv_spec = pl.BlockSpec((1, pairs, UNIT, PAIR), lambda b: (b, 0, 0, 0))
    return pl.pallas_call(
        join_kernel,
        grid=(blocks,),
        in_specs=[
            pl.BlockSpec((UNIT, head_width), lambda b: (b, 0)),
            kv_spec,
            kv_spec,
            pl.BlockSpec((pairs, UNIT, PAIR), lambda b: (0, 0, 0)),
        ]
        + [table_spec] * 3,
        out_specs=[
            pl.BlockSpec((UNIT, 3 * head_width), lambda b: (b, 0)),
            pl.BlockSpec((1, 3 * head_width), lambda b: (0, 0)),
        ],
        out_shape=[
            jax.ShapeDtypeStruct((rows, 3 * head_width), BF),
            jax.ShapeDtypeStruct((1, 3 * head_width), F32),
        ],
        name="join",
    )(dq, own, near, far, *tables)


def up_kernel(x_ref, w_ref, b_ref, hidden_ref, slope_ref):
    rise = dot_nn(x_ref[...], w_ref[...]) + b_ref[...]
    phi = 0.5 + 0.5 * lax.erf(rise * 0.7071067811865476)
    bell = jnp.exp(rise * rise * -0.5) * 0.3989422804014327
    hidden_ref[...] = (rise * phi).astype(BF)
    slope_ref[...] = phi + rise * bell


def up_call(normed, weight, bias):
    rows, width = normed.shape
    cols = weight.shape[1]
    tile = 256
    return pl.pallas_call(
        up_kernel,
        grid=(rows // tile,),
        in_specs=[
            pl.BlockSpec((tile, width), lambda m: (m, 0)),
            pl.BlockSpec((width, cols), lambda m: (0, 0)),
            pl.BlockSpec((1, cols), lambda m: (0, 0)),
        ],
        out_specs=[pl.BlockSpec((tile, cols), lambda m: (m, 0))] * 2,
        out_shape=[
            jax.ShapeDtypeStruct((rows, cols), BF),
            jax.ShapeDtypeStruct((rows, cols), F32),
        ],
        name="up",
    )(normed, weight, bias)


def grad_kernel(side_ref, left_ref, *refs, chunk):
    rights, mine_ref, sent_ref = refs[:-2], refs[-2], refs[-1]
    first = side_ref[0] == 0
    at = 0
    for right_ref in rights:
        cols = slice(at, at + right_ref.shape[1])
        at += right_ref.shape[1]
        product = dot_tn(left_ref[...], right_ref[...])
        for pair in range(product.shape[0] // (2 * chunk)):
            low = product[2 * pair * chunk : (2 * pair + 1) * chunk]
            high = product[(2 * pair + 1) * chunk : (2 * pair + 2) * chunk]
            mine_ref[pair, :, cols] = jnp.where(first, low, high).astype(mine_ref.dtype)
            sent_ref[pair, :, cols] = jnp.where(first, high, low).astype(BF)


def grad_call(side, left, rights, chunk):
    rows, width = left.shape
    cols = sum(right.shape[1] for right in rights)
    tile = max(256, 2 * chunk)
    pairs = tile // (2 * chunk)
    outer = width // (2 * chunk)
    out_spec = pl.BlockSpec((pairs, chunk, cols), lambda m, s: (m, 0, 0))
    return pl.pallas_call(
        functools.partial(grad_kernel, chunk=chunk),
        grid_spec=pltpu.PrefetchScalarGridSpec(
            num_scalar_prefetch=1,
            grid=(width // tile,),
            in_specs=[pl.BlockSpec((rows, tile), lambda m, s: (0, m))]
            + [pl.BlockSpec(right.shape, lambda m, s: (0, 0)) for right in rights],
            out_specs=[out_spec, out_spec],
        ),
        out_shape=[
            jax.ShapeDtypeStruct((outer, chunk, cols), BF),
            jax.ShapeDtypeStruct((outer, chunk, cols), BF),
        ],
        name="weight_grad",
    )(side, left, *rights)


def pair_kernel(at_ref, mine_ref, came_ref, own_ref, *part_refs):
    turn = pl.program_id(0)
    total = mine_ref[0].astype(F32) + came_ref[0].astype(F32)

    @pl.when(turn == 0)
    def _():
        own_ref[...] = total

    for index, part_ref in enumerate(part_refs):

        @pl.when(turn == index + 1)
        def _(part_ref=part_ref):
            part_ref[...] = total.astype(BF)


def pair_call(at, mine, came):
    outer, chunk, cols = mine.shape
    in_spec = pl.BlockSpec((1, chunk, cols), lambda d, a: ((a[0] + d) % outer, 0, 0))
    out_spec = pl.BlockSpec((chunk, cols), lambda d, a: (0, 0))
    return pl.pallas_call(
        pair_kernel,
        grid_spec=pltpu.PrefetchScalarGridSpec(
            num_scalar_prefetch=1,
            grid=(outer,),
            in_specs=[in_spec, in_spec],
            out_specs=[out_spec] * outer,
        ),
        out_shape=[jax.ShapeDtypeStruct((chunk, cols), F32)]
        + [jax.ShapeDtypeStruct((chunk, cols), BF)] * (outer - 1),
        name="pair_sum",
    )(at, mine, came)


def place_kernel(me_ref, own_ref, beside_ref, across_ref, diagonal_ref, out_ref):
    for index, ref in enumerate((own_ref, beside_ref, across_ref, diagonal_ref)):

        @pl.when(pl.program_id(0) == index)
        def _(ref=ref):
            out_ref[...] = ref[...]


def place_call(me, blocks):
    rows, width = blocks[0].shape
    whole = pl.BlockSpec((rows, width), lambda i, m: (0, 0))
    return pl.pallas_call(
        place_kernel,
        grid_spec=pltpu.PrefetchScalarGridSpec(
            num_scalar_prefetch=1,
            grid=(4,),
            in_specs=[whole] * 4,
            out_specs=pl.BlockSpec((rows, width), lambda i, m: (m[0] ^ i, 0)),
        ),
        out_shape=jax.ShapeDtypeStruct((4 * rows, width), blocks[0].dtype),
        name="place",
    )(me, *blocks)


def place_norm_kernel(me_ref, gain_ref, shift_ref, own_ref, beside_ref, across_ref, diagonal_ref, out_ref):
    for index, ref in enumerate((own_ref, beside_ref, across_ref, diagonal_ref)):

        @pl.when(pl.program_id(0) == index)
        def _(ref=ref):
            out_ref[...] = (ref[...].astype(F32) * gain_ref[...] + shift_ref[...]).astype(out_ref.dtype)


def place_norm_call(me, gain, shift, blocks):
    rows, width = blocks[0].shape
    whole = pl.BlockSpec((rows, width), lambda i, m: (0, 0))
    line = pl.BlockSpec((1, width), lambda i, m: (0, 0))
    return pl.pallas_call(
        place_norm_kernel,
        grid_spec=pltpu.PrefetchScalarGridSpec(
            num_scalar_prefetch=1,
            grid=(4,),
            in_specs=[line] * 2 + [whole] * 4,
            out_specs=pl.BlockSpec((rows, width), lambda i, m: (m[0] ^ i, 0)),
        ),
        out_shape=jax.ShapeDtypeStruct((4 * rows, width), blocks[0].dtype),
        name="place_norm",
    )(me, gain, shift, *blocks)


def place_sides_kernel(where_ref, *refs):
    outer = (len(refs) - 1) // 2
    mine, other, out_ref = refs[:outer], refs[outer:-1], refs[-1]
    low = where_ref[1] == 0
    for index in range(outer):

        @pl.when(pl.program_id(0) == index)
        def _(index=index):
            out_ref[0, 0] = jnp.where(low, mine[index][...], other[index][...])
            out_ref[0, 1] = jnp.where(low, other[index][...], mine[index][...])


def place_sides_call(at, side, mine, other):
    outer = len(mine)
    chunk, cols = mine[0].shape
    spec = pl.BlockSpec((chunk, cols), lambda i, w: (0, 0))
    full = pl.pallas_call(
        place_sides_kernel,
        grid_spec=pltpu.PrefetchScalarGridSpec(
            num_scalar_prefetch=1,
            grid=(outer,),
            in_specs=[spec] * (2 * outer),
            out_specs=pl.BlockSpec(
                (1, 2, chunk, cols), lambda i, w: (jnp.where(w[0] < i, w[0] - i + outer, w[0] - i), 0, 0, 0)
            ),
        ),
        out_shape=jax.ShapeDtypeStruct((outer, 2, chunk, cols), mine[0].dtype),
        name="place_sides",
    )(jnp.stack([at, side]), *mine, *other)
    return full.reshape(2 * outer * chunk, cols)


def flipped(count, bit):
    return [(i, i ^ bit) for i in range(count)]


def shifted(count, distance):
    devices = range(count)
    return [(i - distance, i) for i in devices if i - distance in devices]


def rolled_outer(outer, distance):
    return [
        (o * 2 + y, (o + distance) % outer * 2 + y) for o in range(outer) for y in range(2)
    ]


def gather_line(piece):
    outer = lax.axis_size("seq") // 2
    came = [lax.ppermute(piece, "seq", rolled_outer(outer, distance)) for distance in range(1, outer)]
    return [piece] + came


def other_sides(line):
    count = lax.axis_size("seq")
    return [lax.ppermute(shard, "seq", flipped(count, 1)) for shard in line]


def placed(line, other, after=None):
    place = lax.axis_index("seq")
    if after is not None:
        place, _ = lax.optimization_barrier((place, after))
    return place_sides_call(place // 2, place % 2, line, other)


def gather_rows_whole(piece):
    return lax.all_gather(piece, "seq", axis=0, tiled=True)


def scatter_grad(left, rights):
    count = lax.axis_size("seq")
    outer = count // 2
    place = lax.axis_index("seq")
    chunk = left.shape[1] // count
    mine, sent = grad_call((place % 2)[None], left, rights, chunk)
    came = lax.ppermute(sent, "seq", flipped(count, 1))
    total, *parts = pair_call((place // 2)[None], mine, came)
    for distance, part in enumerate(parts, 1):
        total = total + lax.ppermute(part, "seq", rolled_outer(outer, distance)).astype(F32)
    return total


def gather_tokens(rows, gain=None, shift=None):
    count = lax.axis_size("tensor")
    me = lax.axis_index("tensor")
    across = lax.ppermute(rows, "tensor", flipped(count, 2))
    beside = lax.ppermute(rows, "tensor", flipped(count, 1))
    diagonal = lax.ppermute(across, "tensor", flipped(count, 1))
    if gain is not None:
        return place_norm_call(me[None], gain, shift, (rows, beside, across, diagonal))
    return place_call(me[None], (rows, beside, across, diagonal))


def scatter_tokens(partial):
    count = lax.axis_size("tensor")
    me = lax.axis_index("tensor")
    core, chip = me % 2, me // 2
    split = partial.reshape(2, 2, partial.shape[0] // count, partial.shape[1])
    sent = lax.dynamic_index_in_dim(split, 1 - core, 1, keepdims=False)
    kept = lax.dynamic_index_in_dim(split, core, 1, keepdims=False)
    came = lax.ppermute(sent, "tensor", flipped(count, 1))
    far = lax.dynamic_index_in_dim(kept, 1 - chip, 0, keepdims=False).astype(F32)
    far = far + lax.dynamic_index_in_dim(came, 1 - chip, 0, keepdims=False).astype(F32)
    across = lax.ppermute(far.astype(BF), "tensor", flipped(count, 2))
    near = lax.dynamic_index_in_dim(kept, chip, 0, keepdims=False).astype(F32)
    near = near + lax.dynamic_index_in_dim(came, chip, 0, keepdims=False).astype(F32)
    return near + across.astype(F32)


def exchanged(rows):
    return lax.all_to_all(rows, ("seq", "tensor"), 0, 0, tiled=True)


def layer_norm(values, gain, shift):
    center = values - jnp.mean(values, axis=1, keepdims=True)
    scale_inv = lax.rsqrt(jnp.mean(center * center, axis=1, keepdims=True) + EPSILON)
    unit = center * scale_inv
    return (unit * gain + shift, unit, scale_inv)


def norm_back(grad, unit, scale_inv, gain):
    scaled = grad * gain
    return scale_inv * (
        scaled
        - jnp.mean(scaled, axis=1, keepdims=True)
        - unit * jnp.mean(scaled * unit, axis=1, keepdims=True)
    )


def rotary_tables(offsets):
    exponent = jnp.arange(0, ROT, 2).astype(F32) / ROT
    rates = 10000.0 ** (-exponent)
    head = jnp.concatenate([rates, rates, jnp.zeros(HEAD_DIM - ROT, F32)])
    lane = jnp.arange(LANES) % HEAD_DIM
    angles = offsets.astype(F32)[:, None] * jnp.concatenate([head, head])[None, :]
    sine = jnp.sin(angles)
    low = jnp.where(lane < ROT // 2, -sine, 0.0)
    high = jnp.where((lane >= ROT // 2) & (lane < ROT), sine, 0.0)
    return (jnp.cos(angles), low, high)


def local(
    block_input,
    lengths,
    ln_gain,
    ln_bias,
    qkv_weight,
    qkv_bias,
    out_weight,
    up_weight,
    up_bias,
    down_weight,
    out_bias,
    out_grad,
):
    tensor_count = lax.axis_size("tensor")
    seq_count = lax.axis_size("seq")
    everyone = seq_count * tensor_count
    me_tensor = lax.axis_index("tensor")
    own_rows, width = block_input.shape
    group = own_rows * tensor_count
    layers = qkv_weight.shape[0]
    chunk = qkv_weight.shape[1]
    head_width = qkv_weight.shape[3]
    heads = head_width // HEAD_DIM
    hidden_width = up_weight.shape[2]
    first = lax.axis_index("seq") * group
    positions = first + jnp.arange(group, dtype=jnp.int32)
    ends = jnp.cumsum(lengths)
    starts_of = jnp.sum(jnp.where(ends[None, :] <= positions[:, None], lengths[None, :], 0), axis=1)
    offsets = positions - starts_of
    tables = rotary_tables(offsets)
    counts = offsets[::UNIT] // UNIT + 1

    small_sizes = []
    pieces = []
    for array in (ln_gain, ln_bias, out_bias, qkv_bias, up_bias):
        pieces.append(array.reshape(-1))
        small_sizes.append(array.size)
    packed = jnp.concatenate(pieces)
    small = exchanged(jnp.broadcast_to(packed[None, :], (everyone, packed.size)))
    parts = []
    at = 0
    for size in small_sizes:
        parts.append(small[:, at : at + size])
        at += size

    def over_all(part):
        return jnp.transpose(part.reshape(everyone, layers, -1), (1, 0, 2)).reshape(layers, width)

    def over_seq(part):
        part = part.reshape(seq_count, tensor_count, -1)
        return lax.dynamic_index_in_dim(part, me_tensor, 1, keepdims=False)

    gains = over_all(parts[0]).astype(F32)
    shifts = over_all(parts[1]).astype(F32)
    out_biases = over_all(parts[2]).astype(F32)
    per = HEAD_DIM // seq_count
    joint_bias = over_seq(parts[3]).reshape(seq_count, layers, 3, heads, per)
    joint_bias = jnp.transpose(joint_bias, (1, 2, 3, 0, 4)).reshape(layers, 1, 3 * head_width)
    joint_bias = joint_bias.astype(F32)
    groups = up_bias.shape[1]
    rise_bias = over_seq(parts[4]).reshape(seq_count, layers, groups, -1)
    rise_bias = jnp.transpose(rise_bias, (1, 2, 0, 3)).reshape(layers, 1, hidden_width).astype(F32)

    pieces = [
        (
            qkv_weight[layer].reshape(chunk, 3 * head_width),
            up_weight[layer],
            jnp.concatenate([out_weight[layer], down_weight[layer]], axis=1),
        )
        for layer in range(layers)
    ]
    lines, arrived = [], ()
    for piece in pieces[0]:
        if arrived:
            piece, _ = lax.optimization_barrier((piece, arrived))
        lines.append(gather_line(piece))
        arrived = lines[-1][1:]
    weights = [tuple(placed(line, other_sides(line)) for line in lines)]
    others = None

    kept = []
    current = block_input
    for layer in range(layers):
        gain, shift = gains[layer][None], shifts[layer][None]
        normed, unit, scale_inv = layer_norm(current, gain, shift)
        if layer == 0:
            normed_rows = gather_tokens(unit.astype(BF), gain, shift)
        else:
            normed_rows = gather_tokens(normed.astype(BF))
        if layer:
            weights.append(tuple(placed(*pair, normed_rows) for pair in zip(lines, others)))
        qkv_full, up_full, fall_full = weights[layer]
        query, own, tail = qkv_call(normed_rows, qkv_full, joint_bias[layer], tables)
        near = lax.ppermute(own, "seq", shifted(seq_count, 1))
        far = lax.ppermute(tail, "seq", shifted(seq_count, 2))
        if layer + 1 < layers:
            held, _ = lax.optimization_barrier((pieces[layer + 1], (near, far)))
            lines = [gather_line(piece) for piece in held]
            others = [other_sides(line) for line in lines]
        hidden, slope = up_call(normed_rows, up_full, rise_bias[layer])
        mixed, lse = fwd_call(counts, query, own, near, far)
        if GATES and layer + 1 < layers:
            mixed, _ = lax.optimization_barrier((mixed, lines[0][1:]))
        partial = dot_nt(mixed, fall_full[:, :head_width]) + dot_nt(hidden, fall_full[:, head_width:])
        branch = scatter_tokens(partial.astype(BF))
        if GATES and layer + 1 < layers:
            branch, _ = lax.optimization_barrier((branch, others[0]))
        kept.append((normed_rows, unit, scale_inv, query, own, near, far, hidden, slope, mixed, lse))
        current = current + branch + out_biases[layer][None, :]

    gradient = out_grad
    collected = []
    for layer in reversed(range(layers)):
        qkv_full, up_full, fall_full = weights[layer]
        normed_rows, unit, scale_inv, query, own, near, far, hidden, slope, mixed, lse = kept[layer]
        bias_grad = jnp.sum(gradient, axis=0)
        grad_rows = gather_tokens(gradient.astype(BF))
        mixed_grad = dot_nn(grad_rows, fall_full[:, :head_width]).astype(BF)
        whole = WHOLE[layer]
        if not whole:
            fall_grad = scatter_grad(grad_rows, (mixed, hidden))
        dq, down, dnear, dfar = bwd_call(counts, query, own, near, far, mixed, mixed_grad, lse, tables)
        came_near = lax.ppermute(dnear, "seq", shifted(seq_count, -1))
        came_far = lax.ppermute(dfar, "seq", shifted(seq_count, -2))
        hidden_grad = dot_nn(grad_rows, fall_full[:, head_width:])
        rise_grad = (hidden_grad * slope).astype(BF)
        rise_bias_grad = jnp.sum(rise_grad, axis=0, dtype=F32)
        if not whole:
            up_grad = scatter_grad(normed_rows, (rise_grad,))
        normed_part = dot_nt(rise_grad, up_full)
        joint_grad, joint_bias_grad = join_call(dq, down, came_near, came_far, tables)
        if whole:
            every = jnp.concatenate(
                [
                    dot_tn(grad_rows, jnp.concatenate([mixed, hidden], axis=1)).astype(BF),
                    dot_tn(normed_rows, rise_grad).astype(BF),
                    dot_tn(normed_rows, joint_grad).astype(BF),
                ],
                axis=1,
            )
            every = lax.psum_scatter(every, "seq", scatter_dimension=0, tiled=True).astype(F32)
            fall_grad = every[:, : head_width + hidden_width]
            up_grad = every[:, head_width + hidden_width : head_width + 2 * hidden_width]
            joint_weight_grad = every[:, head_width + 2 * hidden_width :]
        else:
            joint_weight_grad = scatter_grad(normed_rows, (joint_grad,))
        normed_part = normed_part + dot_nt(joint_grad, qkv_full)
        normed_grad = scatter_tokens(normed_part.astype(BF))
        gain_grad = jnp.sum(normed_grad * unit, axis=0)
        shift_grad = jnp.sum(normed_grad, axis=0)
        gradient = gradient + norm_back(normed_grad, unit, scale_inv, gains[layer][None, :])
        collected.append(
            (gain_grad, shift_grad, bias_grad, joint_bias_grad.reshape(-1), rise_bias_grad,
             joint_weight_grad, fall_grad, up_grad)
        )
    collected = collected[::-1]

    def stacked(member):
        return jnp.stack([entry[member] for entry in collected])

    def to_all(member):
        value = stacked(member).reshape(layers, everyone, -1)
        return jnp.transpose(value, (1, 0, 2)).reshape(everyone, -1)

    def to_seq(value):
        mine = jnp.arange(tensor_count)[None, :, None] == me_tensor
        return jnp.where(mine, value[:, None, :], 0.0).reshape(everyone, -1)

    joint_out = stacked(3).reshape(layers, 3, heads, seq_count, per)
    joint_out = jnp.transpose(joint_out, (3, 0, 1, 2, 4)).reshape(seq_count, -1)
    rise_out = stacked(4).reshape(layers, groups, seq_count, -1)
    rise_out = jnp.transpose(rise_out, (2, 0, 1, 3)).reshape(seq_count, -1)
    outgoing = jnp.concatenate(
        [to_all(0), to_all(1), to_all(2), to_seq(joint_out), to_seq(rise_out)], axis=1
    )
    summed = jnp.sum(exchanged(outgoing), axis=0)
    results = []
    at = 0
    for array in (ln_gain, ln_bias, out_bias, qkv_bias, up_bias):
        results.append(summed[at : at + array.size].reshape(array.shape))
        at += array.size
    joint_weight_grad = stacked(5).reshape(layers, chunk, 3, head_width)
    fall_grad = stacked(6)
    return (
        current,
        gradient,
        results[0],
        results[1],
        joint_weight_grad,
        results[3],
        fall_grad[:, :, :head_width],
        stacked(7),
        results[4],
        fall_grad[:, :, head_width:],
        results[2],
    )


GATES = True
WHOLE = (False, True)


def solution(mesh):
    tokens = P(("seq", "tensor"), None)
    vector = P(None, ("seq", "tensor"))
    matrix = P(None, "seq", "tensor")
    joint = P(None, "seq", None, "tensor")
    joint_vector = P(None, None, "tensor", "seq")
    rise_vector = P(None, "tensor", "seq")
    in_specs = (
        tokens, P(), vector, vector, joint, joint_vector, matrix, matrix, rise_vector, matrix,
        vector, tokens,
    )
    out_specs = (
        tokens, tokens, vector, vector, joint, joint_vector, matrix, matrix, rise_vector, matrix,
        vector,
    )
    return jax.shard_map(local, mesh=mesh, in_specs=in_specs, out_specs=out_specs, check_vma=False)
```
